128 devices in a mesh: ctx: 16 (over x, y_lo, core), head: 8 (over z, y_hi).
Axes of the slice: x: 4, y: 4 (y_hi: 2, y_lo: 2; y = y_hi * 2 + y_lo), z: 4, core: 2. Of those that a mesh axis runs over, the one named last changes fastest.
Arguments:
- hidden: bfloat16 [32768, 1024], P('ctx'), may hold values from -6 to 6
- norm_gain: float32 [1024], replicated, may hold values from 0.1 to 1.9
- w_zx: bfloat16 [1024, 2, 2048], P(None, None, 'head'), may hold values from -0.1875 to 0.1875
- w_bc: bfloat16 [1024, 256], replicated, may hold values from -0.1875 to 0.1875
- w_dt: bfloat16 [1024, 32], P(None, 'head'), may hold values from -0.1875 to 0.1875
- dt_bias: float32 [32], P('head'), may hold values from -2 to 1
- decay_rate: float32 [32], P('head'), may hold values from 1e-07 to 0.03
- skip_gain: float32 [32], P('head'), may hold values from 0.5 to 2
- conv_x: float32 [4, 2048], P(None, 'head'), may hold values from -3 to 3
- conv_bc: float32 [4, 256], replicated, may hold values from -3 to 3
- w_out: bfloat16 [2048, 1024], P('head'), may hold values from -0.125 to 0.125
Outputs:
- mixed: bfloat16 [32768, 1024], P(('ctx', 'head'))
The draws below stay inside these ranges and needn't reach their ends.
All inputs are finite; a program needn't handle non-finite values.
Results may differ from the reference program's by a relative error of at most 0.013.
Values may be sent and summed in bfloat16 or wider, within the bound.
A program may use at most 128 MiB of HBM per device.

```python
import jax
import jax.numpy as jnp
from jax import lax

D = 1024
HEADS = 32
STATE = 128
CONV = 4
BLOCK = 256
INNER = 2048
LENGTH = 32768


def draw_decay_rate(key, part):
    spread = jax.random.uniform(key, (HEADS,), jnp.float32)
    return jnp.exp(jnp.log(1e-05) + spread * (jnp.log(0.03) - jnp.log(1e-05)))


def block_levels(key, dims, split, low, largest):
    level = 1.0
    for dim, shards_of in split:
        steps = jax.random.uniform(jax.random.fold_in(jax.random.fold_in(key, 6), dim), (shards_of,), jnp.float32, low / len(split), largest / len(split))
        level = level * jnp.repeat(jnp.exp(steps), dims[dim] // shards_of).reshape((-1,) + (1,) * (len(dims) - 1 - dim))
    return level


def gaussian(stream_key, shape, deviation, reach, pieces=(), dtype=jnp.bfloat16):
    array = jax.random.normal(stream_key, shape, jnp.float32) * deviation
    if len(pieces) > 0:
        array = block_levels(stream_key, shape, pieces, -0.22, 0.18) * array
    return jnp.clip(array, min=-reach, max=reach).astype(dtype)


def setup_inputs(seed: int = 0) -> dict:
    key_of = jax.random.split(jax.random.key(seed), 12)
    hidden = gaussian(key_of[0], (LENGTH, D), 1.0, 6.0, ((0, 16),))
    norm_gain = jnp.clip(1.0 + 0.18 * jax.random.normal(key_of[1], (D,), jnp.float32), 0.1, 1.9)
    w_zx = gaussian(key_of[2], (D, 2, INNER), D ** -0.5, 0.1875, ((2, 8),))
    w_bc = gaussian(key_of[3], (D, 2 * STATE), D ** -0.5, 0.1875)
    w_dt = gaussian(key_of[4], (D, HEADS), D ** -0.5, 0.1875, ((1, 8),))
    dt_bias = jnp.clip(-2.0 + 3.0 * jax.random.uniform(key_of[5], (HEADS,), jnp.float32) ** block_levels(key_of[5], (HEADS,), ((0, 8),), -0.2, 0.2), -2.0, 1.0)
    decay_rate = draw_decay_rate(jax.random.fold_in(key_of[11], 71), 0)
    skip_gain = jnp.clip(0.5 + 1.5 * jax.random.uniform(key_of[7], (HEADS,), jnp.float32) ** block_levels(key_of[7], (HEADS,), ((0, 8),), -0.2, 0.2), 0.5, 2.0)
    conv_x = gaussian(key_of[8], (CONV, INNER), 0.5, 3.0, ((1, 8),), jnp.float32)
    conv_bc = gaussian(key_of[9], (CONV, 2 * STATE), 0.5, 3.0, (), jnp.float32)
    w_out = gaussian(key_of[10], (INNER, D), INNER ** -0.5, 0.125, ((0, 8),))
    return {"hidden": hidden, "norm_gain": norm_gain, "w_zx": w_zx, "w_bc": w_bc, "w_dt": w_dt, "dt_bias": dt_bias, "decay_rate": decay_rate, "skip_gain": skip_gain, "conv_x": conv_x, "conv_bc": conv_bc, "w_out": w_out}


epsilon = 1e-05

def normed_rows(rows, norm_gain):
    values = rows.astype(jnp.float32)
    scales = lax.rsqrt(lax.optimization_barrier(jnp.mean(values * values, axis=-1, keepdims=True)) + epsilon)
    return (values * scales * norm_gain).astype(jnp.bfloat16)

def project_rows(normed, w_zx, w_bc, w_dt, dt_bias):
    widths = w_zx.shape[2]
    joined = jnp.dot(normed, w_zx.reshape(w_zx.shape[0], 2 * widths), preferred_element_type=jnp.float32).astype(jnp.bfloat16)
    maps = jnp.dot(normed, w_bc, preferred_element_type=jnp.float32).astype(jnp.bfloat16)
    gates = joined[:, :widths]
    stream = jnp.concatenate([joined[:, widths:], maps], axis=1)
    steps_dt = jax.nn.softplus(jnp.dot(normed, w_dt, preferred_element_type=jnp.float32) + dt_bias)
    return (gates, stream, steps_dt)

def conv_silu(padded, conv_weights, amount):
    summed = jnp.zeros((amount, padded.shape[1]), jnp.float32)
    for lag_index in range(conv_weights.shape[0]):
        summed = summed + conv_weights[lag_index] * padded[lag_index:lag_index + amount].astype(jnp.float32)
    return jax.nn.silu(summed).astype(jnp.bfloat16)

def block_terms(values, b_rows, c_rows, steps_dt, decay_rate):
    cumulated = jnp.cumsum(-decay_rate * steps_dt, axis=1)
    weighted = (values.astype(jnp.float32) * steps_dt[..., None]).astype(jnp.bfloat16)
    scores = jnp.einsum('bsn,brn->bsr', c_rows.astype(jnp.float32), b_rows.astype(jnp.float32))
    across = jnp.swapaxes(cumulated, 1, 2)
    length_block = values.shape[1]
    lower = jnp.arange(length_block)[:, None] >= jnp.arange(length_block)[None, :]
    decays = jnp.exp(jnp.where(lower, across[..., :, None] - across[..., None, :], -jnp.inf))
    mixing = (scores[:, None] * decays).astype(jnp.bfloat16)
    inside = jnp.einsum('bhsr,brhp->bshp', mixing.astype(jnp.float32), weighted.astype(jnp.float32))
    tails = (weighted.astype(jnp.float32) * jnp.exp(cumulated[:, -1:, :] - cumulated)[..., None]).astype(jnp.bfloat16)
    ends = jnp.einsum('brhp,brn->bhpn', tails.astype(jnp.float32), b_rows.astype(jnp.float32))
    return (inside, ends, cumulated)

def carried_part(c_rows, cumulated, entering):
    reads = jnp.einsum('bsn,bhpn->bshp', c_rows.astype(jnp.float32), entering, precision=lax.Precision.HIGHEST)
    return reads * jnp.exp(cumulated)[..., None]

def strand(stream, gates, steps_dt, conv_weights, decay_rate, skip_gain):
    amount = stream.shape[0]
    heads = steps_dt.shape[1]
    inner = gates.shape[1]
    blocks = amount // BLOCK
    padded = jnp.concatenate([jnp.zeros((conv_weights.shape[0] - 1, stream.shape[1]), jnp.bfloat16), stream], axis=0)
    active = conv_silu(padded, conv_weights, amount)
    values = active[:, :inner].reshape(blocks, BLOCK, heads, inner // heads)
    b_rows = active[:, inner:inner + STATE].reshape(blocks, BLOCK, STATE)
    c_rows = active[:, inner + STATE:].reshape(blocks, BLOCK, STATE)
    blocked_dt = steps_dt.reshape(blocks, BLOCK, heads)

    def step_block(carried, inputs):
        values_b, b_block, c_block, dt_block = inputs
        inside, ends, cumulated = block_terms(values_b[None], b_block[None], c_block[None], dt_block[None], decay_rate)
        outputs = inside + carried_part(c_block[None], cumulated, carried[None])
        renewed = jnp.exp(cumulated[0, -1])[:, None, None] * carried + ends[0]
        return (renewed, outputs[0])
    initial = jnp.zeros((heads, inner // heads, STATE), jnp.float32)
    final_state, outputs = lax.scan(step_block, initial, (values, b_rows, c_rows, blocked_dt))
    outputs = outputs.reshape(amount, heads, inner // heads)
    outputs = outputs + skip_gain[:, None] * values.reshape(amount, heads, inner // heads).astype(jnp.float32)
    gated = outputs * jax.nn.silu(gates.astype(jnp.float32)).reshape(amount, heads, inner // heads)
    normed = gated * lax.rsqrt(lax.optimization_barrier(jnp.mean(gated * gated, axis=-1, keepdims=True)) + epsilon)
    return normed.reshape(amount, inner)

def reference(hidden, norm_gain, w_zx, w_bc, w_dt, dt_bias, decay_rate, skip_gain, conv_x, conv_bc, w_out):
    conv_weights = jnp.concatenate([conv_x, conv_bc], axis=1)
    results = []
    for strand_rows in (hidden, hidden[::-1, ::-1]):
        normed = normed_rows(strand_rows, norm_gain)
        gates, stream, steps_dt = project_rows(normed, w_zx, w_bc, w_dt, dt_bias)
        results.append(strand(stream, gates, steps_dt, conv_weights, decay_rate, skip_gain))
    combined = (results[0] + results[1][::-1]).astype(jnp.bfloat16)
    mixed = hidden.astype(jnp.float32) + jnp.dot(combined, w_out, preferred_element_type=jnp.float32)
    return mixed.astype(jnp.bfloat16)
```

```python
import jax
import jax.numpy as jnp
from jax import lax
from jax.experimental import pallas as pl
from jax.experimental.pallas import tpu as pltpu
from jax.sharding import PartitionSpec as P

MESH = pl.DeviceIdType.MESH
F32 = jnp.float32
BF16 = jnp.bfloat16
BLOCK = 256
STATE = 128
HEAD = 64
CTX = 16
GROUP = 8
STAGES = 4
MESSAGE = STATE + 16
LOG2E = 1.4426950408889634
epsilon = 1e-05


def dot(a, b):
    return jnp.dot(a, b, preferred_element_type=F32)


def dot_rows(a, b):
    return lax.dot_general(a, b, (((1,), (1,)), ((), ())), preferred_element_type=F32)


def halves(v):
    high = v.astype(BF16)
    return high, (v - high.astype(F32)).astype(BF16)


def silu(v):
    half = 0.5 * v
    return half + half * jnp.tanh(half)


def softplus(v):
    return jnp.maximum(v, 0.0) + jnp.log1p(jnp.exp(-jnp.abs(v)))


def iotas(shape):
    return lax.broadcasted_iota(jnp.int32, shape, 0), lax.broadcasted_iota(jnp.int32, shape, 1)


def remote(src, dst, send, recv, ctx, head):
    return pltpu.make_async_remote_copy(
        src_ref=src, dst_ref=dst, send_sem=send, recv_sem=recv,
        device_id=(ctx, head), device_id_type=MESH,
    )


def kernel(
    hid, gain, wzx, wbc, wdt, consts, conv, wout, out,
    hbuf, wX, wZ, wo, st, scl, dtb, vb, wb, btb, cb, cum, ec, ent, prow, ins, gb,
    state, arow, xs, xa, msg, rmsg, cbuf, rbuf, acc, low, upp, spread, mean, flip,
    hsem, osem, wsend, wrecv, halo_send, halo_recv, ssend, srecv, csend, crecv,
):
    blocks = hbuf.shape[0]
    inner = vb.shape[3]
    heads = inner // HEAD
    width = inner + 2 * STATE
    ctx = lax.axis_index("ctx")
    me = lax.axis_index("head")
    core = lax.rem(ctx, 2)

    barrier = pltpu.get_barrier_semaphore()
    ctx_peers = [lax.rem(ctx + 1, CTX), lax.rem(ctx + CTX - 1, CTX)]
    for k in range(STAGES):
        bit = lax.rem(lax.div(ctx, 2**k), 2)
        ctx_peers.append(ctx + (1 - 2 * bit) * 2**k)
    head_peers = [lax.rem(me + d, GROUP) for d in range(1, GROUP)]
    for peer in ctx_peers:
        pl.semaphore_signal(barrier, inc=1, device_id=(peer, me), device_id_type=MESH)
    for peer in head_peers:
        pl.semaphore_signal(barrier, inc=1, device_id=(ctx, peer), device_id_type=MESH)

    def load(b):
        return pltpu.make_async_copy(
            hid.at[pl.ds(pl.multiple_of(b * BLOCK, BLOCK), BLOCK), :], hbuf.at[b], hsem.at[b]
        )

    for b in (blocks - 1, *range(blocks - 1)):
        load(b).start()
    own = [
        pltpu.make_async_copy(wout.at[pl.ds(c * 128, 128), :], wo.at[me, c], osem.at[c])
        for c in range(2)
    ]
    for c in range(2):
        own[c].start()

    r0, c0 = iotas((BLOCK, BLOCK))
    low[...] = (r0 >= c0).astype(BF16)
    upp[...] = (r0 <= c0).astype(BF16)
    flip[...] = (r0 + c0 == BLOCK - 1).astype(BF16)
    lane_head = c0 // HEAD
    q0 = lax.rem(r0, 128)
    for s in range(2):
        spread[s] = (q0 == lane_head + s * heads).astype(BF16)
    mean[...] = jnp.where(r0 // HEAD == lane_head, 1.0 / HEAD, 0.0).astype(BF16)

    pieces = wX.shape[0] // BLOCK
    for j in range(pieces):
        span = pl.ds(j * BLOCK, BLOCK)
        back = pl.ds((pieces - 1 - j) * BLOCK, BLOCK)
        column = jnp.concatenate(
            [
                jnp.broadcast_to(gain[pl.ds(2 * j + t, 1), :], (128, 128)).T
                for t in range(2)
            ],
            axis=0,
        )
        gz = (wzx[span, :].astype(F32) * jnp.concatenate([column] * 4, axis=1)).astype(BF16)
        gbc = (wbc[span, :].astype(F32) * jnp.concatenate([column] * 2, axis=1)).astype(BF16)
        gdt = (wdt[span, :].astype(F32) * column).astype(BF16)
        gx = jnp.concatenate([gz[:, inner:], gbc], axis=1)
        turned = dot(flip[...], jnp.concatenate([gx, gz[:, :inner], gdt], axis=1)).astype(BF16)
        wX[span, :width] = gx
        wX[back, width : 2 * width] = turned[:, :width]
        wZ[span, :inner] = gz[:, :inner]
        wZ[back, inner:] = turned[:, width : width + inner]
        mine = lax.broadcasted_iota(jnp.int32, gdt.shape, 1) < heads
        zero = jnp.zeros_like(gdt)
        dtb[j] = jnp.where(mine, gdt, zero).astype(F32)
        scl[pieces - 1 - j] = jnp.where(mine, zero, turned[:, width + inner :]).astype(F32)
    for j in range(pieces):
        wX[pl.ds(j * BLOCK, BLOCK), 2 * width :] = (dtb[j] + scl[j]).astype(BF16)

    pl.semaphore_wait(barrier, len(ctx_peers) + len(head_peers))

    partner = ctx_peers[2]
    across = me + 1 - 2 * lax.rem(me, 2)
    up = lax.rem(me + 2, GROUP)
    down = lax.rem(me + GROUP - 2, GROUP)
    onward = lax.rem(me + 2 + core * 4, GROUP)
    origin = lax.rem(me + 6 - core * 4, GROUP)

    def other(h):
        return h + 1 - 2 * lax.rem(h, 2)

    far = lax.rem(me + 4, GROUP)
    mine_half = wout.at[pl.ds(pl.multiple_of(core * 128, 128), 128), :]
    sources = [across, down, up, other(down), other(up), far, other(far)]

    def slot_copy(src, k, source_here, ctx_to, head_to, send_index):
        return remote(src, wo.at[source_here, core], wsend.at[send_index], wrecv.at[k], ctx_to, head_to)

    w1 = [
        slot_copy(mine_half, 0, me, ctx, across, 0),
        slot_copy(mine_half, 1, me, ctx, up, 1),
        slot_copy(mine_half, 2, me, ctx, down, 2),
    ]
    w2 = [
        slot_copy(wo.at[across, core], 3, across, ctx, up, 3),
        slot_copy(wo.at[across, core], 4, across, ctx, down, 4),
    ]
    w3 = [
        slot_copy(wo.at[origin, core], 5, origin, ctx, onward, 5),
        slot_copy(wo.at[other(origin), core], 6, other(origin), ctx, onward, 6),
    ]
    w4 = [
        remote(wo.at[h, core], wo.at[h, core], wsend.at[7 + k], wrecv.at[7 + k], partner, me)
        for k, h in enumerate(sources)
    ]

    def arrived(k):
        remote(mine_half, wo.at[sources[k], core], wsend.at[0], wrecv.at[k], ctx, me).wait_recv()

    def partner_arrived(k):
        h = sources[k]
        remote(wo.at[h, core], wo.at[h, 1 - core], wsend.at[0], wrecv.at[7 + k], partner, me).wait_recv()

    for copy in w1:
        copy.start()

    rate = consts[1:2, :128]
    bias = consts[0:1, :128]
    skip = consts[2:3, :]

    def first_rows():
        return [
            remote(
                st.at[0, blocks, pl.ds(0, 8), :], st.at[0, 0, pl.ds(0, 8), :],
                halo_send.at[0], halo_recv.at[0], ctx_peers[0], me,
            ),
            remote(
                st.at[1, 0, pl.ds(BLOCK, 8), :], st.at[1, blocks, pl.ds(BLOCK, 8), :],
                halo_send.at[1], halo_recv.at[1], ctx_peers[1], me,
            ),
        ]

    def project(i, carry):
        b = lax.rem(i + blocks - 1, blocks)
        load(b).wait()
        h = hbuf[b]
        hf = h.astype(F32)
        scale = lax.rsqrt(jnp.sum(hf * hf, axis=1, keepdims=True) / h.shape[1] + epsilon)
        p = dot(h, wX[...])
        ahead = p[:, :width] * scale
        st[0, b, 8:, :] = ahead
        st[0, b + 1, 0:8, :] = ahead[BLOCK - 8 :, :]
        behind = p[:, width : 2 * width] * scale
        st[1, b + 1, :BLOCK, :] = behind
        st[1, b, BLOCK:, :] = behind[0:8, :]
        dtb[b] = softplus(p[:, 2 * width :] * scale + bias)
        scl[b] = jnp.broadcast_to(scale, (BLOCK, 128))

        @pl.when(i == 2)
        def _():
            for copy in first_rows():
                copy.start()

        return carry

    lax.fori_loop(0, blocks, project, 0)

    arrived(0)
    for copy in w2:
        copy.start()
    w4[0].start()

    for copy in first_rows():
        copy.wait_recv()
    st[0, 0, 0:8, :] = jnp.where(ctx == 0, 0.0, st[0, 0, 0:8, :])
    st[1, blocks, BLOCK:, :] = jnp.where(ctx == CTX - 1, 0.0, st[1, blocks, BLOCK:, :])

    state[...] = jnp.zeros_like(state)
    arow[...] = jnp.ones_like(arow)

    def local(i, carry):
        for s in range(2):
            b = i if s == 0 else blocks - 1 - i
            total = jnp.zeros((BLOCK, width), F32)
            for k in range(4):
                shift = 5 + k if s == 0 else 3 - k
                total = total + conv[k : k + 1, :] * st[s, b + s, shift : shift + BLOCK, :]
            active = silu(total)
            x = active[:, :inner]
            bt = active[:, inner : inner + STATE].T.astype(BF16)
            btb[s, b] = bt
            cb[s, b] = active[:, inner + STATE :].astype(BF16)
            vb[s, b] = x.astype(BF16)
            dt = dtb[b]
            high, rest = halves(dt * (-LOG2E * rate))
            tri = low[...] if s == 0 else upp[...]
            c = dot(tri, high) + dot(tri, rest)
            cum[s, b] = c
            end = c[BLOCK - 1 : BLOCK, :] if s == 0 else c[0:1, :]
            table = spread[s]
            steps = dot(jnp.concatenate(halves(dt), axis=1), table)
            late = dot(jnp.concatenate(halves(dt * jnp.exp2(end - c)), axis=1), table)
            reach = dot(jnp.concatenate(halves(jnp.exp2(c)), axis=1), table)
            wb[s, b] = (x * steps).astype(BF16)
            ec[s, b] = reach
            ends = dot(bt, (x * late).astype(BF16))
            decay = reach[BLOCK - 1 : BLOCK, :] if s == 0 else reach[0:1, :]
            held = state[s]
            ent[s, b] = held
            state[s] = decay * held + ends
            before = arow[s, 0:1, :]
            prow[s, b] = jnp.broadcast_to(before, (8, inner))
            arow[s] = jnp.broadcast_to(before * decay, (8, inner))
        return carry

    lax.fori_loop(0, blocks, local, 0)

    xs[...] = jnp.zeros_like(xs)
    xa[...] = jnp.ones_like(xa)

    line = lax.broadcasted_iota(jnp.int32, (16, inner), 0)

    def exchange(k):
        return remote(
            msg.at[k], rmsg.at[k], ssend.at[k], srecv.at[k], ctx_peers[2 + k], me
        )

    def send_stage(k):
        for s in range(2):
            msg[k, s, :STATE, :] = state[s].astype(BF16)
            high, rest = halves(arow[s, 0:1, :])
            msg[k, s, STATE:, :] = jnp.where(
                line == 0, high.astype(F32), jnp.where(line == 1, rest.astype(F32), 0.0)
            ).astype(BF16)
        exchange(k).start()

    def merge_stage(k):
        exchange(k).wait_recv()
        bit = lax.rem(lax.div(ctx, 2**k), 2)
        for s in range(2):
            theirs = rmsg[k, s, :STATE, :].astype(F32)
            tail = rmsg[k, s, STATE:, :].astype(F32)
            factor = tail[0:1, :] + tail[1:2, :]
            earlier = bit == 1 - s
            now = state[s]
            mine = arow[s, 0:1, :]
            reach = xa[s, 0:1, :]
            xs[s] = jnp.where(earlier, reach * theirs + xs[s], xs[s])
            xa[s] = jnp.broadcast_to(jnp.where(earlier, reach * factor, reach), (8, inner))
            state[s] = jnp.where(earlier, mine * theirs + now, factor * now + theirs)
            arow[s] = jnp.broadcast_to(mine * factor, (8, inner))

    send_stage(0)

    for k in (1, 2):
        arrived(k)
        w4[k].start()
    arrived(3)
    arrived(4)
    for copy in w3:
        copy.start()
    w4[3].start()
    w4[4].start()

    def within(i, carry):
        for k in range(STAGES - 1):

            @pl.when(i == 2 * k + 2)
            def _():
                merge_stage(k)
                send_stage(k + 1)

        h = hbuf[i]
        scale = scl[i]
        g = silu(dot(h, wZ[...]) * jnp.concatenate([scale] * (2 * inner // 128), axis=1))
        first, second = iotas((BLOCK, BLOCK))
        side = lax.broadcasted_iota(jnp.int32, (BLOCK, 128), 1) < HEAD
        for s in range(2):
            gb[s, i] = g[:, s * inner : (s + 1) * inner]
            keep = first >= second if s == 0 else first <= second
            scores = jnp.where(keep, dot(cb[s, i], btb[s, i]), 0.0)
            c = cum[s, i]
            turned = c.T
            for pair in range(heads // 2):
                parts = []
                for t in range(2):
                    lane = s * heads + pair * 2 + t
                    gap = c[:, lane : lane + 1] - turned[lane : lane + 1, :]
                    mixing = (scores * jnp.exp2(jnp.minimum(gap, 0.0))).astype(BF16)
                    parts.append(dot(mixing, wb[s, i, :, pair * 128 : (pair + 1) * 128]))
                at = slice(pair * 128, (pair + 1) * 128)
                ins[s, i, :, at] = jnp.where(side, parts[0], parts[1]) + skip[:, at] * vb[
                    s, i, :, at
                ].astype(F32)
        return carry

    lax.fori_loop(0, blocks, within, 0)
    merge_stage(STAGES - 1)

    for k in (5, 6):
        arrived(k)
        w4[k].start()

    def finish(i, carry):
        b = lax.rem(me + 1 + i, blocks)
        both = jnp.zeros((BLOCK, inner), F32)
        for s in range(2):
            whole = (ent[s, b] + prow[s, b][0:1, :] * xs[s]).astype(BF16)
            result = ins[s, b] + ec[s, b] * dot(cb[s, b], whole)
            gated = result * gb[s, b]
            power = dot((gated * gated).astype(BF16), mean[...])
            both = both + gated * lax.rsqrt(power + epsilon)
        cbuf[b] = both.astype(BF16)

        @pl.when(i < blocks - 1)
        def _():
            remote(cbuf.at[b], rbuf.at[me], csend.at[b], crecv.at[me], ctx, b).start()

        return carry

    lax.fori_loop(0, blocks, finish, 0)

    for c in range(2):
        own[c].wait()
    for k in range(7):
        partner_arrived(k)

    acc[...] = hbuf[me].astype(F32)

    def multiply(block, j):
        for c in range(2):
            acc[...] += dot(block[:, c * 128 : (c + 1) * 128], wo[j, c])

    multiply(cbuf[me], me)

    def gathered(i, carry):
        j = lax.rem(me + blocks - 1 - i, blocks)
        remote(cbuf.at[j], rbuf.at[j], csend.at[j], crecv.at[j], ctx, j).wait_recv()
        multiply(rbuf[j], j)
        return carry

    lax.fori_loop(0, blocks - 1, gathered, 0)
    out[...] = acc[...].astype(BF16)

    for copy in w1 + w2 + w3 + w4 + first_rows() + [exchange(k) for k in range(STAGES)]:
        copy.wait_send()

    def drained(i, carry):
        j = lax.rem(me + 1 + i, blocks)
        remote(cbuf.at[j], rbuf.at[me], csend.at[j], crecv.at[me], ctx, j).wait_send()
        return carry

    lax.fori_loop(0, blocks - 1, drained, 0)


def on_device(
    hidden, norm_gain, w_zx, w_bc, w_dt, dt_bias, decay_rate, skip_gain, conv_x, conv_bc, w_out
):
    amount, wide = hidden.shape
    inner = conv_x.shape[1]
    heads = w_dt.shape[1]
    width = inner + 2 * STATE
    blocks = amount // BLOCK
    pad = [(0, inner - 2 * heads)]
    consts = jnp.stack(
        [
            jnp.pad(jnp.tile(dt_bias, 2), pad[0]),
            jnp.pad(jnp.tile(decay_rate, 2), pad[0]),
            jnp.repeat(skip_gain, HEAD),
        ]
    )
    wdt = jnp.pad(jnp.concatenate([w_dt, w_dt], axis=1), [(0, 0), (0, 128 - 2 * heads)])
    conv = jnp.concatenate([conv_x, conv_bc], axis=1)
    vmem = pl.BlockSpec(memory_space=pltpu.VMEM)
    hbm = pl.BlockSpec(memory_space=pl.ANY)
    dma = pltpu.SemaphoreType.DMA
    return pl.pallas_call(
        kernel,
        out_shape=jax.ShapeDtypeStruct((BLOCK, wide), BF16),
        in_specs=[hbm, vmem, vmem, vmem, vmem, vmem, vmem, hbm],
        out_specs=vmem,
        scratch_shapes=[
            pltpu.VMEM((blocks, BLOCK, wide), BF16),
            pltpu.VMEM((wide, 2 * width + 128), BF16),
            pltpu.VMEM((wide, 2 * inner), BF16),
            pltpu.VMEM((GROUP, 2, 128, wide), BF16),
            pltpu.VMEM((2, blocks + 1, BLOCK + 8, width), F32),
            pltpu.VMEM((blocks, BLOCK, 128), F32),
            pltpu.VMEM((blocks, BLOCK, 128), F32),
            pltpu.VMEM((2, blocks, BLOCK, inner), BF16),
            pltpu.VMEM((2, blocks, BLOCK, inner), BF16),
            pltpu.VMEM((2, blocks, STATE, BLOCK), BF16),
            pltpu.VMEM((2, blocks, BLOCK, STATE), BF16),
            pltpu.VMEM((2, blocks, BLOCK, 128), F32),
            pltpu.VMEM((2, blocks, BLOCK, inner), F32),
            pltpu.VMEM((2, blocks, STATE, inner), F32),
            pltpu.VMEM((2, blocks, 8, inner), F32),
            pltpu.VMEM((2, blocks, BLOCK, inner), F32),
            pltpu.VMEM((2, blocks, BLOCK, inner), F32),
            pltpu.VMEM((2, STATE, inner), F32),
            pltpu.VMEM((2, 8, inner), F32),
            pltpu.VMEM((2, STATE, inner), F32),
            pltpu.VMEM((2, 8, inner), F32),
            pltpu.VMEM((STAGES, 2, MESSAGE, inner), BF16),
            pltpu.VMEM((STAGES, 2, MESSAGE, inner), BF16),
            pltpu.VMEM((GROUP, BLOCK, inner), BF16),
            pltpu.VMEM((GROUP, BLOCK, inner), BF16),
            pltpu.VMEM((BLOCK, wide), F32),
            pltpu.VMEM((BLOCK, BLOCK), BF16),
            pltpu.VMEM((BLOCK, BLOCK), BF16),
            pltpu.VMEM((2, BLOCK, BLOCK), BF16),
            pltpu.VMEM((BLOCK, BLOCK), BF16),
            pltpu.VMEM((BLOCK, BLOCK), BF16),
            dma((blocks,)),
            dma((2,)),
            dma((14,)),
            dma((14,)),
            dma((2,)),
            dma((2,)),
            dma((STAGES,)),
            dma((STAGES,)),
            dma((GROUP,)),
            dma((GROUP,)),
        ],
        compiler_params=pltpu.CompilerParams(
            collective_id=0, has_side_effects=True, vmem_limit_bytes=63 * 1024 * 1024
        ),
    )(
        hidden,
        norm_gain.reshape(8, wide // 8),
        w_zx.reshape(wide, 2 * inner),
        w_bc,
        wdt,
        consts,
        conv,
        w_out,
    )


def solution(mesh):
    placed = (
        P("ctx", None),
        P(),
        P(None, None, "head"),
        P(),
        P(None, "head"),
        P("head"),
        P("head"),
        P("head"),
        P(None, "head"),
        P(),
        P("head", None),
    )
    return jax.shard_map(
        on_device, mesh=mesh, in_specs=placed, out_specs=P(("ctx", "head"), None), check_vma=False
    )
```

```python
import jax
import jax.numpy as jnp
from jax import lax
from jax.experimental import pallas as pl
from jax.experimental.pallas import tpu as pltpu
from jax.sharding import PartitionSpec as P

MESH = pl.DeviceIdType.MESH
F32 = jnp.float32
BF16 = jnp.bfloat16
BLOCK = 256
STATE = 128
HEAD = 64
CTX = 16
GROUP = 8
MESSAGE = STATE + 16
LOG2E = 1.4426950408889634
epsilon = 1e-05


def dot(a, b):
    return jnp.dot(a, b, preferred_element_type=F32)


def dot_rows(a, b):
    return lax.dot_general(a, b, (((1,), (1,)), ((), ())), preferred_element_type=F32)


def halves(v):
    high = v.astype(BF16)
    return high, (v - high.astype(F32)).astype(BF16)


def silu(v):
    half = 0.5 * v
    return half + half * jnp.tanh(half)


def softplus(v):
    return jnp.maximum(v, 0.0) + jnp.log1p(jnp.exp(-jnp.abs(v)))


def iotas(shape):
    return lax.broadcasted_iota(jnp.int32, shape, 0), lax.broadcasted_iota(jnp.int32, shape, 1)


def remote(src, dst, send, recv, ctx, head):
    return pltpu.make_async_remote_copy(
        src_ref=src, dst_ref=dst, send_sem=send, recv_sem=recv,
        device_id=(ctx, head), device_id_type=MESH,
    )


def kernel(
    hid, gain, wzx_hbm, wbc_hbm, wdt, bias_in, rate_in, skip_in, conv_x, conv_bc, wout, out,
    hbuf, wX, wZ, wo, st, scl, dtb, vb, btb, cb, cum, ec, ent, prow, ins,
    state, arow, xs, xa, msg, rmsg, cbuf, rbuf, acc, low, upp, spread, mean, flip, wzx, wbc, skips, wC, sc,
    hs, ha, ys, ya, hmsg, hrmsg, xmsg, fmsg, frmsg, wsem, hsem, osem, wsend, wrecv, halo_send, halo_recv, ssend, srecv, csend, crecv,
):
    blocks = hbuf.shape[0]
    inner = vb.shape[3]
    heads = inner // HEAD
    width = inner + STATE
    ctx = lax.axis_index("ctx")
    me = lax.axis_index("head")
    core = lax.rem(ctx, 2)

    barrier = pltpu.get_barrier_semaphore()
    ctx_peers = [lax.rem(ctx + 1, CTX), lax.rem(ctx + CTX - 1, CTX)]
    for k in range(2):
        bit = lax.rem(lax.div(ctx, 2**k), 2)
        ctx_peers.append(ctx + (1 - 2 * bit) * 2**k)
    ctx_peers.extend(lax.rem(ctx + 4 * d, CTX) for d in range(1, 4))
    head_peers = [lax.rem(me + d, GROUP) for d in range(1, GROUP)]
    for peer in ctx_peers:
        pl.semaphore_signal(barrier, inc=1, device_id=(peer, me), device_id_type=MESH)
    for peer in head_peers:
        pl.semaphore_signal(barrier, inc=1, device_id=(ctx, peer), device_id_type=MESH)

    def load(b):
        return pltpu.make_async_copy(
            hid.at[pl.ds(pl.multiple_of(b * BLOCK, BLOCK), BLOCK), :], hbuf.at[b], hsem.at[b]
        )

    weights = [
        pltpu.make_async_copy(wzx_hbm, wzx, wsem.at[0]),
        pltpu.make_async_copy(wbc_hbm, wbc, wsem.at[1]),
    ]
    for copy in weights:
        copy.start()
    for b in (blocks - 1, *range(blocks - 1)):
        load(b).start()
    own = pltpu.make_async_copy(wout, wo.at[me], osem.at[0])
    own.start()

    r0, c0 = iotas((BLOCK, BLOCK))
    low[...] = (r0 >= c0).astype(BF16)
    upp[...] = (r0 <= c0).astype(BF16)
    flip[...] = (r0 + c0 == BLOCK - 1).astype(BF16)
    lane_head = c0 // HEAD
    q0 = lax.rem(r0, 128)
    for s in range(2):
        spread[s] = (q0 == lane_head + s * heads).astype(BF16)
    mean[...] = jnp.where(r0 // HEAD == lane_head, 1.0 / HEAD, 0.0).astype(BF16)

    lane = lax.broadcasted_iota(jnp.int32, (1, 128), 1)
    wide_lane = lax.broadcasted_iota(jnp.int32, (1, inner), 1)
    rate = jnp.zeros((1, 128), F32)
    bias = jnp.zeros((1, 128), F32)
    skip = jnp.zeros((1, inner), F32)
    for h in range(heads):
        taken = (lane == h) | (lane == heads + h)
        rate = jnp.where(taken, rate_in[h] * (-LOG2E), rate)
        bias = jnp.where(taken, bias_in[h], bias)
        skip = jnp.where(wide_lane // HEAD == h, skip_in[h], skip)
    skips[...] = jnp.broadcast_to(skip, skips.shape)

    acc[0:128, :] = jnp.zeros((128, acc.shape[1]), F32)
    pieces = wX.shape[0] // BLOCK
    for copy in weights:
        copy.wait()

    def prepare(j, carry):
        span = pl.ds(pl.multiple_of(j * BLOCK, BLOCK), BLOCK)
        back = pl.ds(pl.multiple_of((pieces - 1 - j) * BLOCK, BLOCK), BLOCK)
        lines = [gain[pl.ds(2 * j + t, 1), :] for t in range(2)]
        column = jnp.concatenate(
            [jnp.broadcast_to(line, (128, 128)).T for line in lines], axis=0
        )
        gz = (wzx[span, :].astype(F32) * jnp.concatenate([column] * 4, axis=1)).astype(BF16)
        gbc = (wbc[span, :].astype(F32) * jnp.concatenate([column] * 2, axis=1)).astype(BF16)
        gx = jnp.concatenate([gz[:, inner:], gbc], axis=1)
        turned = dot(flip[...], jnp.concatenate([gx, gz[:, :inner]], axis=1)).astype(BF16)
        wX[span, :width] = gx[:, :width]
        wX[back, width : 2 * width] = turned[:, :width]
        wC[span, :STATE] = gx[:, width:]
        wC[back, STATE:] = turned[:, width : width + STATE]
        wZ[span, :inner] = gz[:, :inner]
        wZ[back, inner:] = turned[:, width + STATE :]
        gdt = (wdt[:, span].astype(F32) * jnp.concatenate(lines, axis=1)).astype(BF16)
        acc[0:heads, span] = gdt.astype(F32)
        acc[heads : 2 * heads, back] = dot(gdt, flip[...])
        return carry

    lax.fori_loop(0, pieces, prepare, 0)
    for j in range(wX.shape[0] // 128):
        span = slice(j * 128, (j + 1) * 128)
        wX[span, 2 * width :] = acc[0:128, span].T.astype(BF16)

    partner = ctx_peers[2]
    across = me + 1 - 2 * lax.rem(me, 2)
    up = lax.rem(me + 2, GROUP)
    down = lax.rem(me + GROUP - 2, GROUP)
    onward = lax.rem(me + 2 + core * 4, GROUP)
    origin = lax.rem(me + 6 - core * 4, GROUP)

    def other(h):
        return h + 1 - 2 * lax.rem(h, 2)

    far = lax.rem(me + 4, GROUP)
    part = pl.ds(pl.multiple_of(core * (inner // 2), 128), inner // 2)
    rest_part = pl.ds(pl.multiple_of((1 - core) * (inner // 2), 128), inner // 2)
    mine_half = wout.at[part, :]
    sources = [across, down, up, other(down), other(up), far, other(far)]

    def slot_copy(src, k, source_here, ctx_to, head_to, send_index):
        return remote(src, wo.at[source_here, part], wsend.at[send_index], wrecv.at[k], ctx_to, head_to)

    w1 = [
        slot_copy(mine_half, 0, me, ctx, across, 0),
        slot_copy(mine_half, 1, me, ctx, up, 1),
        slot_copy(mine_half, 2, me, ctx, down, 2),
    ]
    w2 = [
        slot_copy(wo.at[across, part], 3, across, ctx, up, 3),
        slot_copy(wo.at[across, part], 4, across, ctx, down, 4),
    ]
    w3 = [
        slot_copy(wo.at[origin, part], 5, origin, ctx, onward, 5),
        slot_copy(wo.at[other(origin), part], 6, other(origin), ctx, onward, 6),
    ]
    w4 = [
        remote(wo.at[h, part], wo.at[h, part], wsend.at[7 + k], wrecv.at[7 + k], partner, me)
        for k, h in enumerate(sources)
    ]

    def arrived(k):
        remote(mine_half, wo.at[sources[k], part], wsend.at[0], wrecv.at[k], ctx, me).wait_recv()

    def partner_arrived(k):
        h = sources[k]
        remote(wo.at[h, part], wo.at[h, rest_part], wsend.at[0], wrecv.at[7 + k], partner, me).wait_recv()

    def first_rows():
        return [
            remote(
                st.at[0, blocks, :, pl.ds(0, 8), :], st.at[0, 0, :, pl.ds(0, 8), :],
                halo_send.at[0], halo_recv.at[0], ctx_peers[0], me,
            ),
            remote(
                st.at[1, 0, :, pl.ds(BLOCK, 8), :], st.at[1, blocks, :, pl.ds(BLOCK, 8), :],
                halo_send.at[1], halo_recv.at[1], ctx_peers[1], me,
            ),
        ]

    def map_rows():
        return [
            remote(
                sc.at[0, blocks, pl.ds(0, 8), :], sc.at[0, 0, pl.ds(0, 8), :],
                halo_send.at[2], halo_recv.at[2], ctx_peers[0], me,
            ),
            remote(
                sc.at[1, 0, pl.ds(BLOCK, 8), :], sc.at[1, blocks, pl.ds(BLOCK, 8), :],
                halo_send.at[3], halo_recv.at[3], ctx_peers[1], me,
            ),
        ]

    def convolve(source, shape_taps, s):
        total = None
        for k in range(4):
            shift = 5 + k if s == 0 else 3 - k
            term = shape_taps[k : k + 1, :] * source[shift : shift + BLOCK, :]
            total = term if total is None else total + term
        return silu(total)

    def project(i, carry):
        b = lax.rem(i + blocks - 1, blocks)
        load(b).wait()
        h = hbuf[b]
        hf = h.astype(F32)
        scale = lax.rsqrt(jnp.sum(hf * hf, axis=1, keepdims=True) / h.shape[1] + epsilon)
        p = dot(h, wX[...])
        ahead = p[:, :width] * scale
        behind = p[:, width : 2 * width] * scale
        for t in range(width // 128):
            at = slice(t * 128, (t + 1) * 128)
            st[0, b, t, 8:, :] = ahead[:, at]
            st[0, b + 1, t, 0:8, :] = ahead[BLOCK - 8 :, at]
            st[1, b + 1, t, :BLOCK, :] = behind[:, at]
            st[1, b, t, BLOCK:, :] = behind[0:8, at]
        dtb[b] = softplus(p[:, 2 * width :] * scale + bias)
        scl[b] = jnp.broadcast_to(scale, (BLOCK, 128))

        @pl.when(i == 2)
        def _():
            pl.semaphore_wait(barrier, len(ctx_peers) + len(head_peers))
            for copy in first_rows() + w1:
                copy.start()

        return carry

    lax.fori_loop(0, blocks, project, 0)

    for copy in first_rows():
        copy.wait_recv()
    st[0, 0, :, 0:8, :] = jnp.where(ctx == 0, 0.0, st[0, 0, :, 0:8, :])
    st[1, blocks, :, BLOCK:, :] = jnp.where(ctx == CTX - 1, 0.0, st[1, blocks, :, BLOCK:, :])

    state[...] = jnp.zeros_like(state)
    arow[...] = jnp.ones_like(arow)

    def local(i, carry):
        @pl.when(i == 4)
        def _():
            arrived(0)
            for copy in w2 + w4[:1]:
                copy.start()

        for s in range(2):
            b = i if s == 0 else blocks - 1 - i
            x = jnp.concatenate(
                [
                    convolve(st.at[s, b + s, t], conv_x[:, t * 128 : (t + 1) * 128], s)
                    for t in range(inner // 128)
                ],
                axis=1,
            )
            bt = convolve(st.at[s, b + s, inner // 128], conv_bc[:, :STATE], s).T.astype(BF16)
            btb[s, b] = bt
            vb[s, b] = x.astype(BF16)
            dt = dtb[b]
            high, rest = halves(dt * rate)
            tri = low[...] if s == 0 else upp[...]
            c = dot(tri, high) + dot(tri, rest)
            cum[s, b] = c
            end = c[BLOCK - 1 : BLOCK, :] if s == 0 else c[0:1, :]
            table = spread[s]
            late = dot(jnp.concatenate(halves(dt * jnp.exp2(end - c)), axis=1), table)
            decay = dot(
                jnp.concatenate(halves(jnp.broadcast_to(jnp.exp2(end), (16, 128))), axis=1), table
            )[0:1, :]
            ends = dot(bt, (x * late).astype(BF16))
            held = state[s]
            ent[s, b] = held
            state[s] = decay * held + ends
            before = arow[s, 0:1, :]
            prow[s, b] = jnp.broadcast_to(before, (8, inner))
            arow[s] = jnp.broadcast_to(before * decay, (8, inner))
        return carry

    lax.fori_loop(0, blocks, local, 0)

    xs[...] = jnp.zeros_like(xs)
    xa[...] = jnp.ones_like(xa)

    half = pl.ds(pl.multiple_of(core * 128, 128), 128)
    other_half = pl.ds(pl.multiple_of((1 - core) * 128, 128), 128)

    def packed(row):
        line = lax.broadcasted_iota(jnp.int32, (16, row.shape[1]), 0)
        high, rest = halves(row)
        return jnp.where(
            line == 0, high.astype(F32), jnp.where(line == 1, rest.astype(F32), 0.0)
        ).astype(BF16)

    def unpacked(tail):
        tail = tail.astype(F32)
        return tail[0:1, :] + tail[1:2, :]

    def joined(k, s, theirs, factor, now, now_a, before, before_a):
        earlier = lax.rem(lax.div(ctx, 2**k), 2) == 1 - s
        mine, reach = now_a[s, 0:1, :], before_a[s, 0:1, :]
        state_now = now[s]
        before[s] = jnp.where(earlier, reach * theirs + before[s], before[s])
        before_a[s] = jnp.broadcast_to(
            jnp.where(earlier, reach * factor, reach), before_a.shape[1:]
        )
        now[s] = jnp.where(earlier, mine * theirs + state_now, factor * state_now + theirs)
        now_a[s] = jnp.broadcast_to(mine * factor, now_a.shape[1:])

    place = lax.div(ctx, 4)
    swap = remote(msg, rmsg, ssend.at[0], srecv.at[0], ctx_peers[2], me)
    pairs = remote(hmsg.at[0], hrmsg.at[0], ssend.at[1], srecv.at[1], ctx_peers[3], me)
    along = [
        remote(
            hmsg.at[1, lax.div(place + d, 4)], xmsg.at[d - 1],
            ssend.at[1 + d], srecv.at[1 + d], ctx_peers[3 + d], me,
        )
        for d in range(1, 4)
    ]
    give = remote(fmsg, frmsg, ssend.at[5], srecv.at[5], ctx_peers[2], me)

    for s in range(2):
        msg[s, :STATE, :] = state[s].astype(BF16)
        msg[s, STATE:, :] = packed(arow[s, 0:1, :])
    swap.start()

    def fill_half(k):
        for s in range(2):
            hmsg[k, s, :STATE, :] = hs[s].astype(BF16)
            hmsg[k, s, STATE:, :] = packed(ha[s, 0:1, :])

    def merge_swap():
        swap.wait_recv()
        for s in range(2):
            theirs = rmsg[s, :STATE, :].astype(F32)
            joined(0, s, theirs, unpacked(rmsg[s, STATE:, :]), state, arow, xs, xa)
            hs[s] = state[s, :, half]
            ha[s] = arow[s, :, half]
        ys[...] = jnp.zeros_like(ys)
        ya[...] = jnp.ones_like(ya)
        fill_half(0)
        pairs.start()

    def merge_pairs():
        pairs.wait_recv()
        for s in range(2):
            theirs = hrmsg[0, s, :STATE, :].astype(F32)
            joined(1, s, theirs, unpacked(hrmsg[0, s, STATE:, :]), hs, ha, ys, ya)
        fill_half(1)
        for copy in along:
            copy.start()

    def merge_along():
        for copy in along:
            copy.wait_recv()
        for s in range(2):
            far_state = jnp.zeros((STATE, 128), F32)
            for d in (3, 2, 1) if s == 0 else (1, 2, 3):
                used = place >= d if s == 0 else place < d
                factor = unpacked(xmsg[d - 1, STATE:, :])
                theirs = xmsg[d - 1, :STATE, :].astype(F32)
                far_state = jnp.where(used, factor * far_state + theirs, far_state)
            ys[s] = ya[s, 0:1, :] * far_state + ys[s]
        fmsg[...] = ys[...].astype(BF16)
        give.start()

    def merge_give():
        give.wait_recv()
        for s in range(2):
            xs[s, :, half] = xa[s, 0:1, half] * ys[s] + xs[s, :, half]
            xs[s, :, other_half] = (
                xa[s, 0:1, other_half] * frmsg[s].astype(F32) + xs[s, :, other_half]
            )

    def project_maps(i, carry):
        b = lax.rem(i + blocks - 1, blocks)
        p = dot(hbuf[b], wC[...])
        scale = scl[b]
        ahead = p[:, :STATE] * scale
        sc[0, b, 8:, :] = ahead
        sc[0, b + 1, 0:8, :] = ahead[BLOCK - 8 :, :]
        behind = p[:, STATE:] * scale
        sc[1, b + 1, :BLOCK, :] = behind
        sc[1, b, BLOCK:, :] = behind[0:8, :]

        @pl.when(i == 2)
        def _():
            for copy in map_rows():
                copy.start()

        return carry

    lax.fori_loop(0, blocks, project_maps, 0)

    def within(step, carry):
        i = lax.rem(step + 1, blocks)

        @pl.when(step == 0)
        def _():
            merge_swap()

        @pl.when(step == 1)
        def _():
            for k in range(1, 5):
                arrived(k)
            for copy in w3 + w4[1:5]:
                copy.start()

        @pl.when(step == 3)
        def _():
            merge_pairs()

        @pl.when(step == blocks - 2)
        def _():
            for copy in map_rows():
                copy.wait_recv()
            sc[0, 0, 0:8, :] = jnp.where(ctx == 0, 0.0, sc[0, 0, 0:8, :])
            sc[1, blocks, BLOCK:, :] = jnp.where(ctx == CTX - 1, 0.0, sc[1, blocks, BLOCK:, :])

        dt_pair = jnp.concatenate(halves(dtb[i]), axis=1)
        first, second = iotas((128, 128))
        side = second < HEAD
        for s in range(2):
            c = cum[s, i]
            maps = convolve(sc.at[s, i + s], conv_bc[:, STATE:], s).astype(BF16)
            cb[s, i] = maps
            ec[s, i] = dot(jnp.concatenate(halves(jnp.exp2(c)), axis=1), spread[s])
            weighted = (vb[s, i].astype(F32) * dot(dt_pair, spread[s])).astype(BF16)
            keep = first >= second if s == 0 else first <= second
            scores = dot(maps, btb[s, i])
            corner = [
                jnp.where(keep, scores[:128, :128], 0.0),
                jnp.where(keep, scores[128:, 128:], 0.0),
            ]
            cross = scores[128:, :128] if s == 0 else scores[:128, 128:]
            turned = c.T
            for pair in range(heads // 2):
                at = slice(pair * 128, (pair + 1) * 128)
                short, long = [], []
                for t in range(2):
                    lane = s * heads + pair * 2 + t
                    down_col = [c[:128, lane : lane + 1], c[128:, lane : lane + 1]]
                    row = turned[lane : lane + 1, :]
                    over = [row[:, :128], row[:, 128:]]
                    square = [
                        (corner[q] * jnp.exp2(jnp.minimum(down_col[q] - over[q], 0.0))).astype(BF16)
                        for q in range(2)
                    ]
                    far_off = (cross * jnp.exp2(down_col[1 - s] - over[s])).astype(BF16)
                    short.append(square[s])
                    long.extend([far_off, square[1]] if s == 0 else [square[0], far_off])
                w = weighted[:, at]
                w_rows = [w[:128, :], w[128:, :]]
                zero = jnp.zeros_like(w_rows[0])
                first_head = [jnp.where(side, v, zero) for v in w_rows]
                second_head = [jnp.where(side, zero, v) for v in w_rows]
                brief = dot(
                    jnp.concatenate(short, axis=1),
                    jnp.concatenate([first_head[s], second_head[s]], axis=0),
                )
                full = dot(
                    jnp.concatenate(long, axis=1), jnp.concatenate(first_head + second_head, axis=0)
                )
                result = [brief, full] if s == 0 else [full, brief]
                for q in range(2):
                    down_rows = slice(q * 128, (q + 1) * 128)
                    ins[s, i, down_rows, at] = result[q] + skips[0:1, at] * vb[
                        s, i, down_rows, at
                    ].astype(F32)
        return carry

    lax.fori_loop(0, blocks, within, 0)
    merge_along()
    merge_give()

    def finish(i, carry):
        b = lax.rem(me + 1 + i, blocks)
        both = jnp.zeros((BLOCK, inner), F32)
        scale = jnp.concatenate([scl[b]] * (inner // 128), axis=1)
        h = hbuf[b]
        for s in range(2):
            gate = silu(dot(h, wZ[:, s * inner : (s + 1) * inner]) * scale)
            whole = (ent[s, b] + prow[s, b][0:1, :] * xs[s]).astype(BF16)
            result = ins[s, b] + ec[s, b] * dot(cb[s, b], whole)
            gated = result * gate
            power = dot((gated * gated).astype(BF16), mean[...])
            both = both + gated * lax.rsqrt(power + epsilon)
        cbuf[b] = both.astype(BF16)

        @pl.when(i == 2)
        def _():
            for k in (5, 6):
                arrived(k)
            for copy in w4[5:]:
                copy.start()

        @pl.when(i < blocks - 1)
        def _():
            remote(cbuf.at[b], rbuf.at[me], csend.at[b], crecv.at[me], ctx, b).start()

        return carry

    lax.fori_loop(0, blocks, finish, 0)

    own.wait()
    for k in range(7):
        partner_arrived(k)

    acc[...] = hbuf[me].astype(F32)

    def multiply(block, j):
        acc[...] += dot(block, wo[j])

    multiply(cbuf[me], me)

    def gathered(i, carry):
        j = lax.rem(me + blocks - 1 - i, blocks)
        remote(cbuf.at[j], rbuf.at[j], csend.at[j], crecv.at[j], ctx, j).wait_recv()
        multiply(rbuf[j], j)
        return carry

    lax.fori_loop(0, blocks - 1, gathered, 0)
    out[...] = acc[...].astype(BF16)

    for copy in w1 + w2 + w3 + w4 + first_rows() + map_rows() + [swap, pairs, give] + along:
        copy.wait_send()

    def drained(i, carry):
        j = lax.rem(me + 1 + i, blocks)
        remote(cbuf.at[j], rbuf.at[me], csend.at[j], crecv.at[me], ctx, j).wait_send()
        return carry

    lax.fori_loop(0, blocks - 1, drained, 0)


def on_device(
    hidden, norm_gain, w_zx, w_bc, w_dt, dt_bias, decay_rate, skip_gain, conv_x, conv_bc, w_out
):
    amount, wide = hidden.shape
    inner = conv_x.shape[1]
    heads = w_dt.shape[1]
    width = inner + STATE
    blocks = amount // BLOCK
    vmem = pl.BlockSpec(memory_space=pltpu.VMEM)
    hbm = pl.BlockSpec(memory_space=pl.ANY)
    smem = pl.BlockSpec(memory_space=pltpu.SMEM)
    dma = pltpu.SemaphoreType.DMA
    return pl.pallas_call(
        kernel,
        out_shape=jax.ShapeDtypeStruct((BLOCK, wide), BF16),
        in_specs=[hbm, vmem, hbm, hbm, vmem, smem, smem, smem, vmem, vmem, hbm],
        out_specs=vmem,
        scratch_shapes=[
            pltpu.VMEM((blocks, BLOCK, wide), BF16),
            pltpu.VMEM((wide, 2 * width + 128), BF16),
            pltpu.VMEM((wide, 2 * inner), BF16),
            pltpu.VMEM((GROUP, inner, wide), BF16),
            pltpu.VMEM((2, blocks + 1, width // 128, BLOCK + 8, 128), F32),
            pltpu.VMEM((blocks, BLOCK, 128), F32),
            pltpu.VMEM((blocks, BLOCK, 128), F32),
            pltpu.VMEM((2, blocks, BLOCK, inner), BF16),
            pltpu.VMEM((2, blocks, STATE, BLOCK), BF16),
            pltpu.VMEM((2, blocks, BLOCK, STATE), BF16),
            pltpu.VMEM((2, blocks, BLOCK, 128), F32),
            pltpu.VMEM((2, blocks, BLOCK, inner), F32),
            pltpu.VMEM((2, blocks, STATE, inner), F32),
            pltpu.VMEM((2, blocks, 8, inner), F32),
            pltpu.VMEM((2, blocks, BLOCK, inner), F32),
            pltpu.VMEM((2, STATE, inner), F32),
            pltpu.VMEM((2, 8, inner), F32),
            pltpu.VMEM((2, STATE, inner), F32),
            pltpu.VMEM((2, 8, inner), F32),
            pltpu.VMEM((2, MESSAGE, inner), BF16),
            pltpu.VMEM((2, MESSAGE, inner), BF16),
            pltpu.VMEM((GROUP, BLOCK, inner), BF16),
            pltpu.VMEM((GROUP, BLOCK, inner), BF16),
            pltpu.VMEM((BLOCK, wide), F32),
            pltpu.VMEM((BLOCK, BLOCK), BF16),
            pltpu.VMEM((BLOCK, BLOCK), BF16),
            pltpu.VMEM((2, BLOCK, BLOCK), BF16),
            pltpu.VMEM((BLOCK, BLOCK), BF16),
            pltpu.VMEM((BLOCK, BLOCK), BF16),
            pltpu.VMEM((wide, 2 * inner), BF16),
            pltpu.VMEM((wide, 2 * STATE), BF16),
            pltpu.VMEM((8, inner), F32),
            pltpu.VMEM((wide, 2 * STATE), BF16),
            pltpu.VMEM((2, blocks + 1, BLOCK + 8, STATE), F32),
            pltpu.VMEM((2, STATE, 128), F32),
            pltpu.VMEM((2, 8, 128), F32),
            pltpu.VMEM((2, STATE, 128), F32),
            pltpu.VMEM((2, 8, 128), F32),
            pltpu.VMEM((2, 2, MESSAGE, 128), BF16),
            pltpu.VMEM((1, 2, MESSAGE, 128), BF16),
            pltpu.VMEM((3, MESSAGE, 128), BF16),
            pltpu.VMEM((2, STATE, 128), BF16),
            pltpu.VMEM((2, STATE, 128), BF16),
            dma((2,)),
            dma((blocks,)),
            dma((1,)),
            dma((14,)),
            dma((14,)),
            dma((4,)),
            dma((4,)),
            dma((6,)),
            dma((6,)),
            dma((GROUP,)),
            dma((GROUP,)),
        ],
        compiler_params=pltpu.CompilerParams(
            collective_id=0, has_side_effects=True, vmem_limit_bytes=63 * 1024 * 1024
        ),
    )(
        hidden,
        norm_gain.reshape(8, wide // 8),
        w_zx.reshape(wide, 2 * inner),
        w_bc,
        w_dt.T,
        dt_bias,
        decay_rate,
        skip_gain,
        conv_x,
        conv_bc,
        w_out,
    )


def solution(mesh):
    placed = (
        P("ctx", None),
        P(),
        P(None, None, "head"),
        P(),
        P(None, "head"),
        P("head"),
        P("head"),
        P("head"),
        P(None, "head"),
        P(),
        P("head", None),
    )
    return jax.shard_map(
        on_device, mesh=mesh, in_specs=placed, out_specs=P(("ctx", "head"), None), check_vma=False
    )
```

```python
import jax
import jax.numpy as jnp
from jax import lax
from jax.experimental import pallas as pl
from jax.experimental.pallas import tpu as pltpu
from jax.sharding import PartitionSpec as P

MESH = pl.DeviceIdType.MESH
F32 = jnp.float32
BF16 = jnp.bfloat16
BLOCK = 256
STATE = 128
HEAD = 64
CTX = 16
GROUP = 8
MESSAGE = STATE + 16
LOG2E = 1.4426950408889634
epsilon = 1e-05


def dot(a, b):
    return jnp.dot(a, b, preferred_element_type=F32)


def dot_rows(a, b):
    return lax.dot_general(a, b, (((1,), (1,)), ((), ())), preferred_element_type=F32)


def halves(v):
    high = v.astype(BF16)
    return high, (v - high.astype(F32)).astype(BF16)


def silu(v):
    half = 0.5 * v
    return half + half * jnp.tanh(half)


def softplus(v):
    return jnp.maximum(v, 0.0) + jnp.log1p(jnp.exp(-jnp.abs(v)))


def iotas(shape):
    return lax.broadcasted_iota(jnp.int32, shape, 0), lax.broadcasted_iota(jnp.int32, shape, 1)


def remote(src, dst, send, recv, ctx, head):
    return pltpu.make_async_remote_copy(
        src_ref=src, dst_ref=dst, send_sem=send, recv_sem=recv,
        device_id=(ctx, head), device_id_type=MESH,
    )


def kernel(
    hid, gain, wzx, wbc_hbm, wdt, bias_in, rate_in, skip_in, conv_x, conv_bc, wout, out,
    hbuf, wX, wZ, wo, st, scl, dtb, vb, btb, cb, cum, raw, lateb, endb, ec, ent, prow, ins,
    state, arow, xs, xa, msg, rmsg, cbuf, rbuf, acc, low, upp, spread, mean, flip, wbc, skips, wC, sc,
    hs, ha, ys, ya, hmsg, hrmsg, xmsg, fmsg, frmsg, wsem, hsem, osem, wsend, wrecv, halo_send, halo_recv, ssend, srecv, csend, crecv,
):
    blocks = hbuf.shape[0]
    inner = vb.shape[3]
    heads = inner // HEAD
    width = inner + STATE
    ctx = lax.axis_index("ctx")
    me = lax.axis_index("head")
    core = lax.rem(ctx, 2)

    barrier = pltpu.get_barrier_semaphore()
    ctx_peers = [lax.rem(ctx + 1, CTX), lax.rem(ctx + CTX - 1, CTX)]
    for k in range(2):
        bit = lax.rem(lax.div(ctx, 2**k), 2)
        ctx_peers.append(ctx + (1 - 2 * bit) * 2**k)
    ctx_peers.extend(lax.rem(ctx + 4 * d, CTX) for d in range(1, 4))
    head_peers = [lax.rem(me + d, GROUP) for d in range(1, GROUP)]
    for peer in ctx_peers:
        pl.semaphore_signal(barrier, inc=1, device_id=(peer, me), device_id_type=MESH)
    for peer in head_peers:
        pl.semaphore_signal(barrier, inc=1, device_id=(ctx, peer), device_id_type=MESH)

    def load(b):
        return pltpu.make_async_copy(
            hid.at[pl.ds(pl.multiple_of(b * BLOCK, BLOCK), BLOCK), :], hbuf.at[b], hsem.at[b]
        )

    weights = [
        pltpu.make_async_copy(wbc_hbm.at[span, :], wbc.at[span, :], wsem.at[j])
        for j, span in enumerate(
            pl.ds(n * BLOCK, BLOCK) for n in range(wzx.shape[0] // BLOCK)
        )
    ]
    for copy in weights:
        copy.start()
    for b in (blocks - 1, *range(blocks - 1)):
        load(b).start()
    own = pltpu.make_async_copy(wout, wo.at[me], osem.at[0])
    own.start()

    r0, c0 = iotas((BLOCK, BLOCK))
    low[...] = (r0 >= c0).astype(BF16)
    upp[...] = (r0 <= c0).astype(BF16)
    flip[...] = (r0 + c0 == BLOCK - 1).astype(BF16)
    lane_head = c0 // HEAD
    q0 = lax.rem(r0, 128)
    for s in range(2):
        spread[s] = (q0 == lane_head + s * heads).astype(BF16)
    mean[...] = jnp.where(r0 // HEAD == lane_head, 1.0 / HEAD, 0.0).astype(BF16)

    lane = lax.broadcasted_iota(jnp.int32, (1, 128), 1)
    wide_lane = lax.broadcasted_iota(jnp.int32, (1, inner), 1)
    rate = jnp.zeros((1, 128), F32)
    bias = jnp.zeros((1, 128), F32)
    skip = jnp.zeros((1, inner), F32)
    for h in range(heads):
        taken = (lane == h) | (lane == heads + h)
        rate = jnp.where(taken, rate_in[h] * (-LOG2E), rate)
        bias = jnp.where(taken, bias_in[h], bias)
        skip = jnp.where(wide_lane // HEAD == h, skip_in[h], skip)
    skips[...] = jnp.broadcast_to(skip, skips.shape)

    acc[0:128, :] = jnp.zeros((128, acc.shape[1]), F32)
    pieces = wX.shape[0] // BLOCK
    def prepare(j, carry):
        span = pl.ds(pl.multiple_of(j * BLOCK, BLOCK), BLOCK)
        back = pl.ds(pl.multiple_of((pieces - 1 - j) * BLOCK, BLOCK), BLOCK)
        pltpu.make_async_copy(wbc_hbm.at[span, :], wbc.at[span, :], wsem.at[j]).wait()
        lines = [gain[pl.ds(2 * j + t, 1), :] for t in range(2)]
        column = jnp.concatenate(
            [jnp.broadcast_to(line, (128, 128)).T for line in lines], axis=0
        )
        gz = (wzx[span, :].astype(F32) * jnp.concatenate([column] * 4, axis=1)).astype(BF16)
        gbc = (wbc[span, :].astype(F32) * jnp.concatenate([column] * 2, axis=1)).astype(BF16)
        gx = jnp.concatenate([gz[:, inner:], gbc], axis=1)
        turned = dot(flip[...], jnp.concatenate([gx, gz[:, :inner]], axis=1)).astype(BF16)
        wX[span, :width] = gx[:, :width]
        wX[back, width : 2 * width] = turned[:, :width]
        wC[span, :STATE] = gx[:, width:]
        wC[back, STATE:] = turned[:, width : width + STATE]
        wZ[span, :inner] = gz[:, :inner]
        wZ[back, inner:] = turned[:, width + STATE :]
        gdt = (wdt[:, span].astype(F32) * jnp.concatenate(lines, axis=1)).astype(BF16)
        acc[0:heads, span] = gdt.astype(F32)
        acc[heads : 2 * heads, back] = dot(gdt, flip[...])
        return carry

    lax.fori_loop(0, pieces, prepare, 0)
    for j in range(wX.shape[0] // 128):
        span = slice(j * 128, (j + 1) * 128)
        wX[span, 2 * width :] = acc[0:128, span].T.astype(BF16)

    partner = ctx_peers[2]
    across = me + 1 - 2 * lax.rem(me, 2)
    up = lax.rem(me + 2, GROUP)
    down = lax.rem(me + GROUP - 2, GROUP)
    onward = lax.rem(me + 2 + core * 4, GROUP)
    origin = lax.rem(me + 6 - core * 4, GROUP)

    def other(h):
        return h + 1 - 2 * lax.rem(h, 2)

    far = lax.rem(me + 4, GROUP)
    part = pl.ds(pl.multiple_of(core * (inner // 2), 128), inner // 2)
    rest_part = pl.ds(pl.multiple_of((1 - core) * (inner // 2), 128), inner // 2)
    mine_half = wout.at[part, :]
    sources = [across, down, up, other(down), other(up), far, other(far)]

    def slot_copy(src, k, source_here, ctx_to, head_to, send_index):
        return remote(src, wo.at[source_here, part], wsend.at[send_index], wrecv.at[k], ctx_to, head_to)

    w1 = [
        slot_copy(mine_half, 0, me, ctx, across, 0),
        slot_copy(mine_half, 1, me, ctx, up, 1),
        slot_copy(mine_half, 2, me, ctx, down, 2),
    ]
    w2 = [
        slot_copy(wo.at[across, part], 3, across, ctx, up, 3),
        slot_copy(wo.at[across, part], 4, across, ctx, down, 4),
    ]
    w3 = [
        slot_copy(wo.at[origin, part], 5, origin, ctx, onward, 5),
        slot_copy(wo.at[other(origin), part], 6, other(origin), ctx, onward, 6),
    ]
    w4 = [
        remote(wo.at[h, part], wo.at[h, part], wsend.at[7 + k], wrecv.at[7 + k], partner, me)
        for k, h in enumerate(sources)
    ]

    def arrived(k):
        remote(mine_half, wo.at[sources[k], part], wsend.at[0], wrecv.at[k], ctx, me).wait_recv()

    def partner_arrived(k):
        h = sources[k]
        remote(wo.at[h, part], wo.at[h, rest_part], wsend.at[0], wrecv.at[7 + k], partner, me).wait_recv()

    def first_rows():
        return [
            remote(
                st.at[0, blocks, :, pl.ds(0, 8), :], st.at[0, 0, :, pl.ds(0, 8), :],
                halo_send.at[0], halo_recv.at[0], ctx_peers[0], me,
            ),
            remote(
                st.at[1, 0, :, pl.ds(BLOCK, 8), :], st.at[1, blocks, :, pl.ds(BLOCK, 8), :],
                halo_send.at[1], halo_recv.at[1], ctx_peers[1], me,
            ),
        ]

    def map_rows():
        return [
            remote(
                sc.at[0, blocks, pl.ds(0, 8), :], sc.at[0, 0, pl.ds(0, 8), :],
                halo_send.at[2], halo_recv.at[2], ctx_peers[0], me,
            ),
            remote(
                sc.at[1, 0, pl.ds(BLOCK, 8), :], sc.at[1, blocks, pl.ds(BLOCK, 8), :],
                halo_send.at[3], halo_recv.at[3], ctx_peers[1], me,
            ),
        ]

    def convolve(source, shape_taps, s):
        total = None
        for k in range(4):
            shift = 5 + k if s == 0 else 3 - k
            term = (0.5 * shape_taps[k : k + 1, :]) * source[shift : shift + BLOCK, :]
            total = term if total is None else total + term
        return total + total * jnp.tanh(total)

    def settle(b):
        dt = softplus(raw[b])
        dtb[b] = dt
        parts = jnp.concatenate(halves(dt * rate), axis=1)
        ahead = dot(low[...], parts)
        behind = dot(upp[...], parts)
        forward = lax.broadcasted_iota(jnp.int32, (BLOCK, 128), 1) < heads
        c = jnp.where(
            forward, ahead[:, :128] + ahead[:, 128:], behind[:, :128] + behind[:, 128:]
        )
        cum[b] = c
        end = jnp.where(forward[0:1, :], c[BLOCK - 1 : BLOCK, :], c[0:1, :])
        lateb[b] = jnp.concatenate(halves(dt * jnp.exp2(end - c)), axis=1)
        endb[b] = jnp.concatenate(halves(jnp.broadcast_to(jnp.exp2(end), (16, 128))), axis=1)

    def project(i, carry):
        b = lax.rem(i + blocks - 1, blocks)
        load(b).wait()
        h = hbuf[b]
        hf = h.astype(F32)
        scale = lax.rsqrt(jnp.sum(hf * hf, axis=1, keepdims=True) / h.shape[1] + epsilon)
        ahead = dot(h, wX[:, :width]) * scale
        p = dot(h, wX[:, width:])
        behind = p[:, :width] * scale
        for t in range(width // 128):
            at = slice(t * 128, (t + 1) * 128)
            st[0, b, t, 8:, :] = ahead[:, at]
            st[0, b + 1, t, 0:8, :] = ahead[BLOCK - 8 :, at]
            st[1, b + 1, t, :BLOCK, :] = behind[:, at]
            st[1, b, t, BLOCK:, :] = behind[0:8, at]
        raw[b] = p[:, width:] * scale + bias
        scl[b] = jnp.broadcast_to(scale, (BLOCK, 128))

        @pl.when(i == 1)
        def _():
            pl.semaphore_wait(barrier, len(ctx_peers) + len(head_peers))
            for copy in first_rows() + w1:
                copy.start()

        return carry

    lax.fori_loop(0, blocks, project, 0)

    def settle_two(i, carry):
        for u in range(4):
            settle(4 * i + u)
        return carry

    lax.fori_loop(0, blocks // 4, settle_two, 0)

    for copy in first_rows():
        copy.wait_recv()
    st[0, 0, :, 0:8, :] = jnp.where(ctx == 0, 0.0, st[0, 0, :, 0:8, :])
    st[1, blocks, :, BLOCK:, :] = jnp.where(ctx == CTX - 1, 0.0, st[1, blocks, :, BLOCK:, :])

    state[...] = jnp.zeros_like(state)
    arow[...] = jnp.ones_like(arow)

    def local(i, carry):
        @pl.when(i == 4)
        def _():
            arrived(0)
            for copy in w2 + w4[:1]:
                copy.start()

        for s in range(2):
            b = i if s == 0 else blocks - 1 - i
            x = jnp.concatenate(
                [
                    convolve(st.at[s, b + s, t], conv_x[:, t * 128 : (t + 1) * 128], s)
                    for t in range(inner // 128)
                ],
                axis=1,
            )
            bt = convolve(st.at[s, b + s, inner // 128], conv_bc[:, :STATE], s).T.astype(BF16)
            btb[s, b] = bt
            vb[s, b] = x.astype(BF16)
            late = dot(lateb[b], spread[s])
            decay = dot(endb[b], spread[s])[0:1, :]
            ends = dot(bt, (x * late).astype(BF16))
            held = state[s]
            ent[s, b] = held
            state[s] = decay * held + ends
            before = arow[s, 0:1, :]
            prow[s, b] = jnp.broadcast_to(before, (8, inner))
            arow[s] = jnp.broadcast_to(before * decay, (8, inner))
        return carry

    lax.fori_loop(0, blocks, local, 0)

    xs[...] = jnp.zeros_like(xs)
    xa[...] = jnp.ones_like(xa)

    half = pl.ds(pl.multiple_of(core * 128, 128), 128)
    other_half = pl.ds(pl.multiple_of((1 - core) * 128, 128), 128)

    def packed(row):
        line = lax.broadcasted_iota(jnp.int32, (16, row.shape[1]), 0)
        high, rest = halves(row)
        return jnp.where(
            line == 0, high.astype(F32), jnp.where(line == 1, rest.astype(F32), 0.0)
        ).astype(BF16)

    def unpacked(tail):
        tail = tail.astype(F32)
        return tail[0:1, :] + tail[1:2, :]

    def joined(k, s, theirs, factor, now, now_a, before, before_a):
        earlier = lax.rem(lax.div(ctx, 2**k), 2) == 1 - s
        mine, reach = now_a[s, 0:1, :], before_a[s, 0:1, :]
        state_now = now[s]
        before[s] = jnp.where(earlier, reach * theirs + before[s], before[s])
        before_a[s] = jnp.broadcast_to(
            jnp.where(earlier, reach * factor, reach), before_a.shape[1:]
        )
        now[s] = jnp.where(earlier, mine * theirs + state_now, factor * state_now + theirs)
        now_a[s] = jnp.broadcast_to(mine * factor, now_a.shape[1:])

    place = lax.div(ctx, 4)
    swap = remote(msg, rmsg, ssend.at[0], srecv.at[0], ctx_peers[2], me)
    pairs = remote(hmsg.at[0], hrmsg.at[0], ssend.at[1], srecv.at[1], ctx_peers[3], me)
    along = [
        remote(
            hmsg.at[1, lax.div(place + d, 4)], xmsg.at[d - 1],
            ssend.at[1 + d], srecv.at[1 + d], ctx_peers[3 + d], me,
        )
        for d in range(1, 4)
    ]
    give = remote(fmsg, frmsg, ssend.at[5], srecv.at[5], ctx_peers[2], me)

    for s in range(2):
        msg[s, :STATE, :] = state[s].astype(BF16)
        msg[s, STATE:, :] = packed(arow[s, 0:1, :])
    swap.start()

    def fill_half(k):
        for s in range(2):
            hmsg[k, s, :STATE, :] = hs[s].astype(BF16)
            hmsg[k, s, STATE:, :] = packed(ha[s, 0:1, :])

    def merge_swap():
        swap.wait_recv()
        for s in range(2):
            theirs = rmsg[s, :STATE, :].astype(F32)
            joined(0, s, theirs, unpacked(rmsg[s, STATE:, :]), state, arow, xs, xa)
            hs[s] = state[s, :, half]
            ha[s] = arow[s, :, half]
        ys[...] = jnp.zeros_like(ys)
        ya[...] = jnp.ones_like(ya)
        fill_half(0)
        pairs.start()

    def merge_pairs():
        pairs.wait_recv()
        for s in range(2):
            theirs = hrmsg[0, s, :STATE, :].astype(F32)
            joined(1, s, theirs, unpacked(hrmsg[0, s, STATE:, :]), hs, ha, ys, ya)
        fill_half(1)
        for copy in along:
            copy.start()

    def merge_along():
        for copy in along:
            copy.wait_recv()
        for s in range(2):
            far_state = jnp.zeros((STATE, 128), F32)
            for d in (3, 2, 1) if s == 0 else (1, 2, 3):
                used = place >= d if s == 0 else place < d
                factor = unpacked(xmsg[d - 1, STATE:, :])
                theirs = xmsg[d - 1, :STATE, :].astype(F32)
                far_state = jnp.where(used, factor * far_state + theirs, far_state)
            ys[s] = ya[s, 0:1, :] * far_state + ys[s]
        fmsg[...] = ys[...].astype(BF16)
        give.start()

    def merge_give():
        give.wait_recv()
        for s in range(2):
            xs[s, :, half] = xa[s, 0:1, half] * ys[s] + xs[s, :, half]
            xs[s, :, other_half] = (
                xa[s, 0:1, other_half] * frmsg[s].astype(F32) + xs[s, :, other_half]
            )

    def project_maps(i, carry):
        b = lax.rem(i + blocks - 1, blocks)
        p = dot(hbuf[b], wC[...])
        scale = scl[b]
        ahead = p[:, :STATE] * scale
        sc[0, b, 8:, :] = ahead
        sc[0, b + 1, 0:8, :] = ahead[BLOCK - 8 :, :]
        behind = p[:, STATE:] * scale
        sc[1, b + 1, :BLOCK, :] = behind
        sc[1, b, BLOCK:, :] = behind[0:8, :]

        @pl.when(i == 2)
        def _():
            for copy in map_rows():
                copy.start()

        @pl.when(i == 6)
        def _():
            merge_swap()

        return carry

    lax.fori_loop(0, blocks, project_maps, 0)

    def within(step, carry):
        i = lax.rem(step + 1, blocks)

        @pl.when(step == 2)
        def _():
            for k in range(1, 5):
                arrived(k)
            for copy in w3 + w4[1:5]:
                copy.start()

        @pl.when(step == 3)
        def _():
            merge_pairs()

        @pl.when(step == blocks - 2)
        def _():
            for copy in map_rows():
                copy.wait_recv()
            sc[0, 0, 0:8, :] = jnp.where(ctx == 0, 0.0, sc[0, 0, 0:8, :])
            sc[1, blocks, BLOCK:, :] = jnp.where(ctx == CTX - 1, 0.0, sc[1, blocks, BLOCK:, :])

        dt_pair = jnp.concatenate(halves(dtb[i]), axis=1)
        first, second = iotas((128, 128))
        side = second < HEAD
        for s in range(2):
            c = cum[i]
            maps = convolve(sc.at[s, i + s], conv_bc[:, STATE:], s).astype(BF16)
            cb[s, i] = maps
            ec[s, i] = dot(jnp.concatenate(halves(jnp.exp2(c)), axis=1), spread[s])
            weighted = (vb[s, i].astype(F32) * dot(dt_pair, spread[s])).astype(BF16)
            keep = first >= second if s == 0 else first <= second
            scores = dot(maps, btb[s, i])
            corner = [
                jnp.where(keep, scores[:128, :128], 0.0),
                jnp.where(keep, scores[128:, 128:], 0.0),
            ]
            cross = scores[128:, :128] if s == 0 else scores[:128, 128:]
            turned = c.T
            for pair in range(heads // 2):
                at = slice(pair * 128, (pair + 1) * 128)
                short, long = [], []
                for t in range(2):
                    lane = s * heads + pair * 2 + t
                    down_col = [c[:128, lane : lane + 1], c[128:, lane : lane + 1]]
                    row = turned[lane : lane + 1, :]
                    over = [row[:, :128], row[:, 128:]]
                    square = [
                        (corner[q] * jnp.exp2(jnp.minimum(down_col[q] - over[q], 0.0))).astype(BF16)
                        for q in range(2)
                    ]
                    far_off = (cross * jnp.exp2(down_col[1 - s] - over[s])).astype(BF16)
                    short.append(square[s])
                    long.extend([far_off, square[1]] if s == 0 else [square[0], far_off])
                w = weighted[:, at]
                w_rows = [w[:128, :], w[128:, :]]
                zero = jnp.zeros_like(w_rows[0])
                first_head = [jnp.where(side, v, zero) for v in w_rows]
                second_head = [jnp.where(side, zero, v) for v in w_rows]
                brief = dot(
                    jnp.concatenate(short, axis=1),
                    jnp.concatenate([first_head[s], second_head[s]], axis=0),
                )
                full = dot(
                    jnp.concatenate(long, axis=1), jnp.concatenate(first_head + second_head, axis=0)
                )
                result = [brief, full] if s == 0 else [full, brief]
                for q in range(2):
                    down_rows = slice(q * 128, (q + 1) * 128)
                    ins[s, i, down_rows, at] = result[q] + skips[0:1, at] * vb[
                        s, i, down_rows, at
                    ].astype(F32)
        return carry

    lax.fori_loop(0, blocks, within, 0)
    merge_along()
    merge_give()

    def finish(i, carry):
        b = lax.rem(me + 1 + i, blocks)
        both = jnp.zeros((BLOCK, inner), F32)
        scale = jnp.concatenate([scl[b]] * (inner // 128), axis=1)
        h = hbuf[b]
        for s in range(2):
            gate = silu(dot(h, wZ[:, s * inner : (s + 1) * inner]) * scale)
            whole = (ent[s, b] + prow[s, b][0:1, :] * xs[s]).astype(BF16)
            result = ins[s, b] + ec[s, b] * dot(cb[s, b], whole)
            gated = result * gate
            power = dot((gated * gated).astype(BF16), mean[...])
            both = both + gated * lax.rsqrt(power + epsilon)
        cbuf[b] = both.astype(BF16)

        @pl.when(i == 2)
        def _():
            for k in (5, 6):
                arrived(k)
            for copy in w4[5:]:
                copy.start()

        @pl.when(i < blocks - 1)
        def _():
            remote(cbuf.at[b], rbuf.at[me], csend.at[b], crecv.at[me], ctx, b).start()

        return carry

    lax.fori_loop(0, blocks, finish, 0)

    own.wait()
    for k in range(7):
        partner_arrived(k)

    acc[...] = hbuf[me].astype(F32)

    def multiply(block, j):
        acc[...] += dot(block, wo[j])

    multiply(cbuf[me], me)

    def gathered(i, carry):
        j = lax.rem(me + blocks - 1 - i, blocks)
        remote(cbuf.at[j], rbuf.at[j], csend.at[j], crecv.at[j], ctx, j).wait_recv()
        multiply(rbuf[j], j)
        return carry

    lax.fori_loop(0, blocks - 1, gathered, 0)
    out[...] = acc[...].astype(BF16)

    for copy in w1 + w2 + w3 + w4 + first_rows() + map_rows() + [swap, pairs, give] + along:
        copy.wait_send()

    def drained(i, carry):
        j = lax.rem(me + 1 + i, blocks)
        remote(cbuf.at[j], rbuf.at[me], csend.at[j], crecv.at[me], ctx, j).wait_send()
        return carry

    lax.fori_loop(0, blocks - 1, drained, 0)


def on_device(
    hidden, norm_gain, w_zx, w_bc, w_dt, dt_bias, decay_rate, skip_gain, conv_x, conv_bc, w_out
):
    amount, wide = hidden.shape
    inner = conv_x.shape[1]
    heads = w_dt.shape[1]
    width = inner + STATE
    blocks = amount // BLOCK
    vmem = pl.BlockSpec(memory_space=pltpu.VMEM)
    hbm = pl.BlockSpec(memory_space=pl.ANY)
    smem = pl.BlockSpec(memory_space=pltpu.SMEM)
    dma = pltpu.SemaphoreType.DMA
    return pl.pallas_call(
        kernel,
        out_shape=pltpu.VMEM((BLOCK, wide), BF16),
        in_specs=[hbm, vmem, vmem, hbm, vmem, smem, smem, smem, vmem, vmem, hbm],
        out_specs=vmem,
        scratch_shapes=[
            pltpu.VMEM((blocks, BLOCK, wide), BF16),
            pltpu.VMEM((wide, 2 * width + 128), BF16),
            pltpu.VMEM((wide, 2 * inner), BF16),
            pltpu.VMEM((GROUP, inner, wide), BF16),
            pltpu.VMEM((2, blocks + 1, width // 128, BLOCK + 8, 128), F32),
            pltpu.VMEM((blocks, BLOCK, 128), F32),
            pltpu.VMEM((blocks, BLOCK, 128), F32),
            pltpu.VMEM((2, blocks, BLOCK, inner), BF16),
            pltpu.VMEM((2, blocks, STATE, BLOCK), BF16),
            pltpu.VMEM((2, blocks, BLOCK, STATE), BF16),
            pltpu.VMEM((blocks, BLOCK, 128), F32),
            pltpu.VMEM((blocks, BLOCK, 128), F32),
            pltpu.VMEM((blocks, BLOCK, 256), BF16),
            pltpu.VMEM((blocks, 16, 256), BF16),
            pltpu.VMEM((2, blocks, BLOCK, inner), F32),
            pltpu.VMEM((2, blocks, STATE, inner), F32),
            pltpu.VMEM((2, blocks, 8, inner), F32),
            pltpu.VMEM((2, blocks, BLOCK, inner), F32),
            pltpu.VMEM((2, STATE, inner), F32),
            pltpu.VMEM((2, 8, inner), F32),
            pltpu.VMEM((2, STATE, inner), F32),
            pltpu.VMEM((2, 8, inner), F32),
            pltpu.VMEM((2, MESSAGE, inner), BF16),
            pltpu.VMEM((2, MESSAGE, inner), BF16),
            pltpu.VMEM((GROUP, BLOCK, inner), BF16),
            pltpu.VMEM((GROUP, BLOCK, inner), BF16),
            pltpu.VMEM((BLOCK, wide), F32),
            pltpu.VMEM((BLOCK, BLOCK), BF16),
            pltpu.VMEM((BLOCK, BLOCK), BF16),
            pltpu.VMEM((2, BLOCK, BLOCK), BF16),
            pltpu.VMEM((BLOCK, BLOCK), BF16),
            pltpu.VMEM((BLOCK, BLOCK), BF16),
            pltpu.VMEM((wide, 2 * STATE), BF16),
            pltpu.VMEM((8, inner), F32),
            pltpu.VMEM((wide, 2 * STATE), BF16),
            pltpu.VMEM((2, blocks + 1, BLOCK + 8, STATE), F32),
            pltpu.VMEM((2, STATE, 128), F32),
            pltpu.VMEM((2, 8, 128), F32),
            pltpu.VMEM((2, STATE, 128), F32),
            pltpu.VMEM((2, 8, 128), F32),
            pltpu.VMEM((2, 2, MESSAGE, 128), BF16),
            pltpu.VMEM((1, 2, MESSAGE, 128), BF16),
            pltpu.VMEM((3, MESSAGE, 128), BF16),
            pltpu.VMEM((2, STATE, 128), BF16),
            pltpu.VMEM((2, STATE, 128), BF16),
            dma((wide // BLOCK,)),
            dma((blocks,)),
            dma((1,)),
            dma((14,)),
            dma((14,)),
            dma((4,)),
            dma((4,)),
            dma((6,)),
            dma((6,)),
            dma((GROUP,)),
            dma((GROUP,)),
        ],
        compiler_params=pltpu.CompilerParams(
            collective_id=0, has_side_effects=True, vmem_limit_bytes=56 * 1024 * 1024
        ),
    )(
        hidden,
        norm_gain.reshape(8, wide // 8),
        pltpu.with_memory_space_constraint(w_zx.reshape(wide, 2 * inner), pltpu.VMEM),
        w_bc,
        w_dt.T,
        dt_bias,
        decay_rate,
        skip_gain,
        conv_x,
        conv_bc,
        w_out,
    )


def solution(mesh):
    placed = (
        P("ctx", None),
        P(),
        P(None, None, "head"),
        P(),
        P(None, "head"),
        P("head"),
        P("head"),
        P("head"),
        P(None, "head"),
        P(),
        P("head", None),
    )
    return jax.shard_map(
        on_device, mesh=mesh, in_specs=placed, out_specs=P(("ctx", "head"), None), check_vma=False
    )
```

```python
import jax
import jax.numpy as jnp
from jax import lax
from jax.experimental import pallas as pl
from jax.experimental.pallas import tpu as pltpu
from jax.sharding import PartitionSpec as P

MESH = pl.DeviceIdType.MESH
F32 = jnp.float32
BF16 = jnp.bfloat16
BLOCK = 256
STATE = 128
HEAD = 64
CTX = 16
GROUP = 8
MESSAGE = STATE + 16
LOG2E = 1.4426950408889634
epsilon = 1e-05


def dot(a, b):
    return jnp.dot(a, b, preferred_element_type=F32)


def dot_rows(a, b):
    return lax.dot_general(a, b, (((1,), (1,)), ((), ())), preferred_element_type=F32)


def halves(v):
    high = v.astype(BF16)
    return high, (v - high.astype(F32)).astype(BF16)


def silu(v):
    half = 0.5 * v
    return half + half * jnp.tanh(half)


def softplus(v):
    return jnp.maximum(v, 0.0) + jnp.log1p(jnp.exp(-jnp.abs(v)))


def iotas(shape):
    return lax.broadcasted_iota(jnp.int32, shape, 0), lax.broadcasted_iota(jnp.int32, shape, 1)


def remote(src, dst, send, recv, ctx, head):
    return pltpu.make_async_remote_copy(
        src_ref=src, dst_ref=dst, send_sem=send, recv_sem=recv,
        device_id=(ctx, head), device_id_type=MESH,
    )


def kernel(
    hid, gain, wzx, wbc_hbm, wdt, bias_in, rate_in, skip_in, conv_x, conv_bc, wout, out,
    hbuf, wX, wZ, wo, st, scl, dtb, vb, btb, cb, cum, raw, lateb, endb, ec, ent, prow, ins,
    state, arow, xs, xa, msg, rmsg, cbuf, rbuf, acc, low, upp, spread, mean, flip, wbc, skips, wC, sc,
    hs, ha, ys, ya, hmsg, hrmsg, xmsg, fmsg, frmsg, wsem, hsem, osem, wsend, wrecv, halo_send, halo_recv, ssend, srecv, csend, crecv,
):
    blocks = hbuf.shape[0]
    inner = vb.shape[3]
    heads = inner // HEAD
    width = inner + STATE
    ctx = lax.axis_index("ctx")
    me = lax.axis_index("head")
    core = lax.rem(ctx, 2)

    barrier = pltpu.get_barrier_semaphore()
    ctx_peers = [lax.rem(ctx + 1, CTX), lax.rem(ctx + CTX - 1, CTX)]
    for k in range(2):
        bit = lax.rem(lax.div(ctx, 2**k), 2)
        ctx_peers.append(ctx + (1 - 2 * bit) * 2**k)
    ctx_peers.extend(lax.rem(ctx + 4 * d, CTX) for d in range(1, 4))
    head_peers = [lax.rem(me + d, GROUP) for d in range(1, GROUP)]
    for peer in ctx_peers:
        pl.semaphore_signal(barrier, inc=1, device_id=(peer, me), device_id_type=MESH)
    for peer in head_peers:
        pl.semaphore_signal(barrier, inc=1, device_id=(ctx, peer), device_id_type=MESH)

    def load(b):
        return pltpu.make_async_copy(
            hid.at[pl.ds(pl.multiple_of(b * BLOCK, BLOCK), BLOCK), :], hbuf.at[b], hsem.at[b]
        )

    weights = [
        pltpu.make_async_copy(wbc_hbm.at[span, :], wbc.at[span, :], wsem.at[j])
        for j, span in enumerate(
            pl.ds(n * BLOCK, BLOCK) for n in range(wzx.shape[0] // BLOCK)
        )
    ]
    for copy in weights:
        copy.start()
    for b in (blocks - 1, *range(blocks - 1)):
        load(b).start()
    own = pltpu.make_async_copy(wout, wo.at[me], osem.at[0])
    own.start()

    r0, c0 = iotas((BLOCK, BLOCK))
    low[...] = (r0 >= c0).astype(BF16)
    upp[...] = (r0 <= c0).astype(BF16)
    flip[...] = (r0 + c0 == BLOCK - 1).astype(BF16)
    lane_head = c0 // HEAD
    q0 = lax.rem(r0, 128)
    for s in range(2):
        spread[s] = (q0 == lane_head + s * heads).astype(BF16)
    mean[...] = jnp.where(r0 // HEAD == lane_head, 1.0 / HEAD, 0.0).astype(BF16)

    lane = lax.broadcasted_iota(jnp.int32, (1, 128), 1)
    wide_lane = lax.broadcasted_iota(jnp.int32, (1, inner), 1)
    rate = jnp.zeros((1, 128), F32)
    bias = jnp.zeros((1, 128), F32)
    skip = jnp.zeros((1, inner), F32)
    for h in range(heads):
        taken = (lane == h) | (lane == heads + h)
        rate = jnp.where(taken, rate_in[h] * (-LOG2E), rate)
        bias = jnp.where(taken, bias_in[h], bias)
        skip = jnp.where(wide_lane // HEAD == h, skip_in[h], skip)
    skips[...] = jnp.broadcast_to(skip, skips.shape)

    acc[0:128, :] = jnp.zeros((128, acc.shape[1]), F32)
    pieces = wX.shape[0] // BLOCK
    def prepare(j, carry):
        span = pl.ds(pl.multiple_of(j * BLOCK, BLOCK), BLOCK)
        back = pl.ds(pl.multiple_of((pieces - 1 - j) * BLOCK, BLOCK), BLOCK)
        pltpu.make_async_copy(wbc_hbm.at[span, :], wbc.at[span, :], wsem.at[j]).wait()
        lines = [gain[pl.ds(2 * j + t, 1), :] for t in range(2)]
        column = jnp.concatenate(
            [jnp.broadcast_to(line, (128, 128)).T for line in lines], axis=0
        )
        gz = (wzx[span, :].astype(F32) * jnp.concatenate([column] * 4, axis=1)).astype(BF16)
        gbc = (wbc[span, :].astype(F32) * jnp.concatenate([column] * 2, axis=1)).astype(BF16)
        gx = jnp.concatenate([gz[:, inner:], gbc], axis=1)
        turned = dot(flip[...], jnp.concatenate([gx, gz[:, :inner]], axis=1)).astype(BF16)
        wX[span, :width] = gx[:, :width]
        wX[back, width : 2 * width] = turned[:, :width]
        wC[span, :STATE] = gx[:, width:]
        wC[back, STATE:] = turned[:, width : width + STATE]
        wZ[span, :inner] = gz[:, :inner]
        wZ[back, inner:] = turned[:, width + STATE :]
        gdt = (wdt[:, span].astype(F32) * jnp.concatenate(lines, axis=1)).astype(BF16)
        acc[0:heads, span] = gdt.astype(F32)
        acc[heads : 2 * heads, back] = dot(gdt, flip[...])
        return carry

    lax.fori_loop(0, pieces, prepare, 0)
    for j in range(wX.shape[0] // 128):
        span = slice(j * 128, (j + 1) * 128)
        wX[span, 2 * width :] = acc[0:128, span].T.astype(BF16)

    partner = ctx_peers[2]
    across = me + 1 - 2 * lax.rem(me, 2)
    up = lax.rem(me + 2, GROUP)
    down = lax.rem(me + GROUP - 2, GROUP)
    onward = lax.rem(me + 2 + core * 4, GROUP)
    origin = lax.rem(me + 6 - core * 4, GROUP)

    def other(h):
        return h + 1 - 2 * lax.rem(h, 2)

    far = lax.rem(me + 4, GROUP)
    part = pl.ds(pl.multiple_of(core * (inner // 2), 128), inner // 2)
    rest_part = pl.ds(pl.multiple_of((1 - core) * (inner // 2), 128), inner // 2)
    mine_half = wout.at[part, :]
    sources = [across, down, up, other(down), other(up), far, other(far)]

    def slot_copy(src, k, source_here, ctx_to, head_to, send_index):
        return remote(src, wo.at[source_here, part], wsend.at[send_index], wrecv.at[k], ctx_to, head_to)

    w1 = [
        slot_copy(mine_half, 0, me, ctx, across, 0),
        slot_copy(mine_half, 1, me, ctx, up, 1),
        slot_copy(mine_half, 2, me, ctx, down, 2),
    ]
    w2 = [
        slot_copy(wo.at[across, part], 3, across, ctx, up, 3),
        slot_copy(wo.at[across, part], 4, across, ctx, down, 4),
    ]
    w3 = [
        slot_copy(wo.at[origin, part], 5, origin, ctx, onward, 5),
        slot_copy(wo.at[other(origin), part], 6, other(origin), ctx, onward, 6),
    ]
    w4 = [
        remote(wo.at[h, part], wo.at[h, part], wsend.at[7 + k], wrecv.at[7 + k], partner, me)
        for k, h in enumerate(sources)
    ]

    def arrived(k):
        remote(mine_half, wo.at[sources[k], part], wsend.at[0], wrecv.at[k], ctx, me).wait_recv()

    def partner_arrived(k):
        h = sources[k]
        remote(wo.at[h, part], wo.at[h, rest_part], wsend.at[0], wrecv.at[7 + k], partner, me).wait_recv()

    def first_rows():
        return [
            remote(
                st.at[0, blocks, :, pl.ds(0, 8), :], st.at[0, 0, :, pl.ds(0, 8), :],
                halo_send.at[0], halo_recv.at[0], ctx_peers[0], me,
            ),
            remote(
                st.at[1, 0, :, pl.ds(BLOCK, 8), :], st.at[1, blocks, :, pl.ds(BLOCK, 8), :],
                halo_send.at[1], halo_recv.at[1], ctx_peers[1], me,
            ),
        ]

    def map_rows():
        return [
            remote(
                sc.at[0, blocks, pl.ds(0, 8), :], sc.at[0, 0, pl.ds(0, 8), :],
                halo_send.at[2], halo_recv.at[2], ctx_peers[0], me,
            ),
            remote(
                sc.at[1, 0, pl.ds(BLOCK, 8), :], sc.at[1, blocks, pl.ds(BLOCK, 8), :],
                halo_send.at[3], halo_recv.at[3], ctx_peers[1], me,
            ),
        ]

    def convolve(source, shape_taps, s):
        total = None
        for k in range(4):
            shift = 5 + k if s == 0 else 3 - k
            term = (0.5 * shape_taps[k : k + 1, :]) * source[shift : shift + BLOCK, :]
            total = term if total is None else total + term
        return total + total * jnp.tanh(total)

    def settle(b):
        dt = softplus(raw[b])
        dtb[b] = dt
        parts = jnp.concatenate(halves(dt * rate), axis=1)
        ahead = dot(low[...], parts)
        behind = dot(upp[...], parts)
        forward = lax.broadcasted_iota(jnp.int32, (BLOCK, 128), 1) < heads
        c = jnp.where(
            forward, ahead[:, :128] + ahead[:, 128:], behind[:, :128] + behind[:, 128:]
        )
        cum[b] = c
        end = jnp.where(forward[0:1, :], c[BLOCK - 1 : BLOCK, :], c[0:1, :])
        lateb[b] = jnp.concatenate(halves(dt * jnp.exp2(end - c)), axis=1)
        endb[b] = jnp.concatenate(halves(jnp.broadcast_to(jnp.exp2(end), (16, 128))), axis=1)

    def project(i, carry):
        b = lax.rem(i + blocks - 1, blocks)
        load(b).wait()
        h = hbuf[b]
        hf = h.astype(F32)
        scale = lax.rsqrt(jnp.sum(hf * hf, axis=1, keepdims=True) / h.shape[1] + epsilon)
        ahead = dot(h, wX[:, :width]) * scale
        p = dot(h, wX[:, width:])
        behind = p[:, :width] * scale
        for t in range(width // 128):
            at = slice(t * 128, (t + 1) * 128)
            st[0, b, t, 8:, :] = ahead[:, at]
            st[0, b + 1, t, 0:8, :] = ahead[BLOCK - 8 :, at]
            st[1, b + 1, t, :BLOCK, :] = behind[:, at]
            st[1, b, t, BLOCK:, :] = behind[0:8, at]
        raw[b] = p[:, width:] * scale + bias
        scl[b] = jnp.broadcast_to(scale, (BLOCK, 128))

        @pl.when(i == 1)
        def _():
            pl.semaphore_wait(barrier, len(ctx_peers) + len(head_peers))
            for copy in first_rows() + w1:
                copy.start()

        return carry

    lax.fori_loop(0, blocks, project, 0)

    def settle_two(i, carry):
        for u in range(4):
            settle(4 * i + u)
        return carry

    lax.fori_loop(0, blocks // 4, settle_two, 0)

    for copy in first_rows():
        copy.wait_recv()
    st[0, 0, :, 0:8, :] = jnp.where(ctx == 0, 0.0, st[0, 0, :, 0:8, :])
    st[1, blocks, :, BLOCK:, :] = jnp.where(ctx == CTX - 1, 0.0, st[1, blocks, :, BLOCK:, :])

    state[...] = jnp.zeros_like(state)
    arow[...] = jnp.ones_like(arow)

    def local(i, carry):
        @pl.when(i == 6)
        def _():
            arrived(0)
            for copy in w2 + w4[:1]:
                copy.start()

        for s in range(2):
            b = i if s == 0 else blocks - 1 - i
            x = jnp.concatenate(
                [
                    convolve(st.at[s, b + s, t], conv_x[:, t * 128 : (t + 1) * 128], s)
                    for t in range(inner // 128)
                ],
                axis=1,
            )
            bt = convolve(st.at[s, b + s, inner // 128], conv_bc[:, :STATE], s).T.astype(BF16)
            btb[s, b] = bt
            vb[s, b] = x.astype(BF16)
            late = dot(lateb[b], spread[s])
            decay = dot(endb[b], spread[s])[0:1, :]
            ends = dot(bt, (x * late).astype(BF16))
            held = state[s]
            ent[s, b] = held
            state[s] = decay * held + ends
            before = arow[s, 0:1, :]
            prow[s, b] = jnp.broadcast_to(before, (8, inner))
            arow[s] = jnp.broadcast_to(before * decay, (8, inner))
        return carry

    lax.fori_loop(0, blocks, local, 0)

    xs[...] = jnp.zeros_like(xs)
    xa[...] = jnp.ones_like(xa)

    half = pl.ds(pl.multiple_of(core * 128, 128), 128)
    other_half = pl.ds(pl.multiple_of((1 - core) * 128, 128), 128)

    def packed(row):
        line = lax.broadcasted_iota(jnp.int32, (16, row.shape[1]), 0)
        high, rest = halves(row)
        return jnp.where(
            line == 0, high.astype(F32), jnp.where(line == 1, rest.astype(F32), 0.0)
        ).astype(BF16)

    def unpacked(tail):
        tail = tail.astype(F32)
        return tail[0:1, :] + tail[1:2, :]

    def joined(k, s, theirs, factor, now, now_a, before, before_a):
        earlier = lax.rem(lax.div(ctx, 2**k), 2) == 1 - s
        mine, reach = now_a[s, 0:1, :], before_a[s, 0:1, :]
        state_now = now[s]
        before[s] = jnp.where(earlier, reach * theirs + before[s], before[s])
        before_a[s] = jnp.broadcast_to(
            jnp.where(earlier, reach * factor, reach), before_a.shape[1:]
        )
        now[s] = jnp.where(earlier, mine * theirs + state_now, factor * state_now + theirs)
        now_a[s] = jnp.broadcast_to(mine * factor, now_a.shape[1:])

    place = lax.div(ctx, 4)
    swap = remote(msg, rmsg, ssend.at[0], srecv.at[0], ctx_peers[2], me)
    pairs = remote(hmsg.at[0], hrmsg.at[0], ssend.at[1], srecv.at[1], ctx_peers[3], me)
    along = [
        remote(
            hmsg.at[1, lax.div(place + d, 4)], xmsg.at[d - 1],
            ssend.at[1 + d], srecv.at[1 + d], ctx_peers[3 + d], me,
        )
        for d in range(1, 4)
    ]
    give = remote(fmsg, frmsg, ssend.at[5], srecv.at[5], ctx_peers[2], me)

    for s in range(2):
        msg[s, :STATE, :] = state[s].astype(BF16)
        msg[s, STATE:, :] = packed(arow[s, 0:1, :])
    swap.start()

    def fill_half(k):
        for s in range(2):
            hmsg[k, s, :STATE, :] = hs[s].astype(BF16)
            hmsg[k, s, STATE:, :] = packed(ha[s, 0:1, :])

    def merge_swap():
        swap.wait_recv()
        for s in range(2):
            theirs = rmsg[s, :STATE, :].astype(F32)
            joined(0, s, theirs, unpacked(rmsg[s, STATE:, :]), state, arow, xs, xa)
            hs[s] = state[s, :, half]
            ha[s] = arow[s, :, half]
        ys[...] = jnp.zeros_like(ys)
        ya[...] = jnp.ones_like(ya)
        fill_half(0)
        pairs.start()

    def merge_pairs():
        pairs.wait_recv()
        for s in range(2):
            theirs = hrmsg[0, s, :STATE, :].astype(F32)
            joined(1, s, theirs, unpacked(hrmsg[0, s, STATE:, :]), hs, ha, ys, ya)
        fill_half(1)
        for copy in along:
            copy.start()

    def merge_along():
        for copy in along:
            copy.wait_recv()
        for s in range(2):
            far_state = jnp.zeros((STATE, 128), F32)
            for d in (3, 2, 1) if s == 0 else (1, 2, 3):
                used = place >= d if s == 0 else place < d
                factor = unpacked(xmsg[d - 1, STATE:, :])
                theirs = xmsg[d - 1, :STATE, :].astype(F32)
                far_state = jnp.where(used, factor * far_state + theirs, far_state)
            ys[s] = ya[s, 0:1, :] * far_state + ys[s]
        fmsg[...] = ys[...].astype(BF16)
        give.start()

    def merge_give():
        give.wait_recv()
        for s in range(2):
            xs[s, :, half] = xa[s, 0:1, half] * ys[s] + xs[s, :, half]
            xs[s, :, other_half] = (
                xa[s, 0:1, other_half] * frmsg[s].astype(F32) + xs[s, :, other_half]
            )

    def project_maps(i, carry):
        b = lax.rem(i + blocks - 1, blocks)
        p = dot(hbuf[b], wC[...])
        scale = scl[b]
        ahead = p[:, :STATE] * scale
        sc[0, b, 8:, :] = ahead
        sc[0, b + 1, 0:8, :] = ahead[BLOCK - 8 :, :]
        behind = p[:, STATE:] * scale
        sc[1, b + 1, :BLOCK, :] = behind
        sc[1, b, BLOCK:, :] = behind[0:8, :]

        @pl.when(i == 2)
        def _():
            for copy in map_rows():
                copy.start()

        @pl.when(i == 6)
        def _():
            merge_swap()

        return carry

    lax.fori_loop(0, blocks, project_maps, 0)

    def within(step, carry):
        i = lax.rem(step + 1, blocks)

        @pl.when(step == 4)
        def _():
            for k in range(1, 5):
                arrived(k)
            for copy in w3 + w4[1:5]:
                copy.start()

        @pl.when(step == 3)
        def _():
            merge_pairs()

        @pl.when(step == blocks - 2)
        def _():
            for copy in map_rows():
                copy.wait_recv()
            sc[0, 0, 0:8, :] = jnp.where(ctx == 0, 0.0, sc[0, 0, 0:8, :])
            sc[1, blocks, BLOCK:, :] = jnp.where(ctx == CTX - 1, 0.0, sc[1, blocks, BLOCK:, :])

        dt_pair = jnp.concatenate(halves(dtb[i]), axis=1)
        first, second = iotas((128, 128))
        side = second < HEAD
        for s in range(2):
            c = cum[i]
            maps = convolve(sc.at[s, i + s], conv_bc[:, STATE:], s).astype(BF16)
            cb[s, i] = maps
            ec[s, i] = dot(jnp.concatenate(halves(jnp.exp2(c)), axis=1), spread[s])
            weighted = (vb[s, i].astype(F32) * dot(dt_pair, spread[s])).astype(BF16)
            keep = first >= second if s == 0 else first <= second
            scores = dot(maps, btb[s, i])
            corner = [
                jnp.where(keep, scores[:128, :128], 0.0),
                jnp.where(keep, scores[128:, 128:], 0.0),
            ]
            cross = scores[128:, :128] if s == 0 else scores[:128, 128:]
            turned = c.T
            for pair in range(heads // 2):
                at = slice(pair * 128, (pair + 1) * 128)
                short, long = [], []
                for t in range(2):
                    lane = s * heads + pair * 2 + t
                    down_col = [c[:128, lane : lane + 1], c[128:, lane : lane + 1]]
                    row = turned[lane : lane + 1, :]
                    over = [row[:, :128], row[:, 128:]]
                    square = [
                        (corner[q] * jnp.exp2(jnp.minimum(down_col[q] - over[q], 0.0))).astype(BF16)
                        for q in range(2)
                    ]
                    far_off = (cross * jnp.exp2(down_col[1 - s] - over[s])).astype(BF16)
                    short.append(square[s])
                    long.extend([far_off, square[1]] if s == 0 else [square[0], far_off])
                w = weighted[:, at]
                w_rows = [w[:128, :], w[128:, :]]
                zero = jnp.zeros_like(w_rows[0])
                first_head = [jnp.where(side, v, zero) for v in w_rows]
                second_head = [jnp.where(side, zero, v) for v in w_rows]
                brief = dot(
                    jnp.concatenate(short, axis=1),
                    jnp.concatenate([first_head[s], second_head[s]], axis=0),
                )
                full = dot(
                    jnp.concatenate(long, axis=1), jnp.concatenate(first_head + second_head, axis=0)
                )
                result = [brief, full] if s == 0 else [full, brief]
                for q in range(2):
                    down_rows = slice(q * 128, (q + 1) * 128)
                    ins[s, i, down_rows, at] = result[q] + skips[0:1, at] * vb[
                        s, i, down_rows, at
                    ].astype(F32)
        return carry

    lax.fori_loop(0, blocks, within, 0)
    merge_along()
    merge_give()

    def finish(i, carry):
        b = lax.rem(me + 1 + i, blocks)
        both = jnp.zeros((BLOCK, inner), F32)
        scale = jnp.concatenate([scl[b]] * (inner // 128), axis=1)
        h = hbuf[b]
        for s in range(2):
            gate = silu(dot(h, wZ[:, s * inner : (s + 1) * inner]) * scale)
            whole = (ent[s, b] + prow[s, b][0:1, :] * xs[s]).astype(BF16)
            result = ins[s, b] + ec[s, b] * dot(cb[s, b], whole)
            gated = result * gate
            power = dot((gated * gated).astype(BF16), mean[...])
            both = both + gated * lax.rsqrt(power + epsilon)
        cbuf[b] = both.astype(BF16)

        @pl.when(i == 4)
        def _():
            for k in (5, 6):
                arrived(k)
            for copy in w4[5:]:
                copy.start()

        @pl.when(i < blocks - 1)
        def _():
            remote(cbuf.at[b], rbuf.at[me], csend.at[b], crecv.at[me], ctx, b).start()

        return carry

    lax.fori_loop(0, blocks, finish, 0)

    own.wait()
    for k in range(7):
        partner_arrived(k)

    acc[...] = hbuf[me].astype(F32)

    def multiply(block, j):
        acc[...] += dot(block, wo[j])

    multiply(cbuf[me], me)

    def gathered(i, carry):
        j = lax.rem(me + blocks - 1 - i, blocks)
        remote(cbuf.at[j], rbuf.at[j], csend.at[j], crecv.at[j], ctx, j).wait_recv()
        multiply(rbuf[j], j)
        return carry

    lax.fori_loop(0, blocks - 1, gathered, 0)
    out[...] = acc[...].astype(BF16)

    for copy in w1 + w2 + w3 + w4 + first_rows() + map_rows() + [swap, pairs, give] + along:
        copy.wait_send()

    def drained(i, carry):
        j = lax.rem(me + 1 + i, blocks)
        remote(cbuf.at[j], rbuf.at[me], csend.at[j], crecv.at[me], ctx, j).wait_send()
        return carry

    lax.fori_loop(0, blocks - 1, drained, 0)


def on_device(
    hidden, norm_gain, w_zx, w_bc, w_dt, dt_bias, decay_rate, skip_gain, conv_x, conv_bc, w_out
):
    amount, wide = hidden.shape
    inner = conv_x.shape[1]
    heads = w_dt.shape[1]
    width = inner + STATE
    blocks = amount // BLOCK
    vmem = pl.BlockSpec(memory_space=pltpu.VMEM)
    hbm = pl.BlockSpec(memory_space=pl.ANY)
    smem = pl.BlockSpec(memory_space=pltpu.SMEM)
    dma = pltpu.SemaphoreType.DMA
    return pl.pallas_call(
        kernel,
        out_shape=pltpu.VMEM((BLOCK, wide), BF16),
        in_specs=[hbm, vmem, vmem, hbm, vmem, smem, smem, smem, vmem, vmem, hbm],
        out_specs=vmem,
        scratch_shapes=[
            pltpu.VMEM((blocks, BLOCK, wide), BF16),
            pltpu.VMEM((wide, 2 * width + 128), BF16),
            pltpu.VMEM((wide, 2 * inner), BF16),
            pltpu.VMEM((GROUP, inner, wide), BF16),
            pltpu.VMEM((2, blocks + 1, width // 128, BLOCK + 8, 128), F32),
            pltpu.VMEM((blocks, BLOCK, 128), F32),
            pltpu.VMEM((blocks, BLOCK, 128), F32),
            pltpu.VMEM((2, blocks, BLOCK, inner), BF16),
            pltpu.VMEM((2, blocks, STATE, BLOCK), BF16),
            pltpu.VMEM((2, blocks, BLOCK, STATE), BF16),
            pltpu.VMEM((blocks, BLOCK, 128), F32),
            pltpu.VMEM((blocks, BLOCK, 128), F32),
            pltpu.VMEM((blocks, BLOCK, 256), BF16),
            pltpu.VMEM((blocks, 16, 256), BF16),
            pltpu.VMEM((2, blocks, BLOCK, inner), F32),
            pltpu.VMEM((2, blocks, STATE, inner), F32),
            pltpu.VMEM((2, blocks, 8, inner), F32),
            pltpu.VMEM((2, blocks, BLOCK, inner), F32),
            pltpu.VMEM((2, STATE, inner), F32),
            pltpu.VMEM((2, 8, inner), F32),
            pltpu.VMEM((2, STATE, inner), F32),
            pltpu.VMEM((2, 8, inner), F32),
            pltpu.VMEM((2, MESSAGE, inner), BF16),
            pltpu.VMEM((2, MESSAGE, inner), BF16),
            pltpu.VMEM((GROUP, BLOCK, inner), BF16),
            pltpu.VMEM((GROUP, BLOCK, inner), BF16),
            pltpu.VMEM((BLOCK, wide), F32),
            pltpu.VMEM((BLOCK, BLOCK), BF16),
            pltpu.VMEM((BLOCK, BLOCK), BF16),
            pltpu.VMEM((2, BLOCK, BLOCK), BF16),
            pltpu.VMEM((BLOCK, BLOCK), BF16),
            pltpu.VMEM((BLOCK, BLOCK), BF16),
            pltpu.VMEM((wide, 2 * STATE), BF16),
            pltpu.VMEM((8, inner), F32),
            pltpu.VMEM((wide, 2 * STATE), BF16),
            pltpu.VMEM((2, blocks + 1, BLOCK + 8, STATE), F32),
            pltpu.VMEM((2, STATE, 128), F32),
            pltpu.VMEM((2, 8, 128), F32),
            pltpu.VMEM((2, STATE, 128), F32),
            pltpu.VMEM((2, 8, 128), F32),
            pltpu.VMEM((2, 2, MESSAGE, 128), BF16),
            pltpu.VMEM((1, 2, MESSAGE, 128), BF16),
            pltpu.VMEM((3, MESSAGE, 128), BF16),
            pltpu.VMEM((2, STATE, 128), BF16),
            pltpu.VMEM((2, STATE, 128), BF16),
            dma((wide // BLOCK,)),
            dma((blocks,)),
            dma((1,)),
            dma((14,)),
            dma((14,)),
            dma((4,)),
            dma((4,)),
            dma((6,)),
            dma((6,)),
            dma((GROUP,)),
            dma((GROUP,)),
        ],
        compiler_params=pltpu.CompilerParams(
            collective_id=0, has_side_effects=True, vmem_limit_bytes=56 * 1024 * 1024
        ),
    )(
        hidden,
        norm_gain.reshape(8, wide // 8),
        pltpu.with_memory_space_constraint(w_zx.reshape(wide, 2 * inner), pltpu.VMEM),
        w_bc,
        w_dt.T,
        dt_bias,
        decay_rate,
        skip_gain,
        conv_x,
        conv_bc,
        w_out,
    )


def solution(mesh):
    placed = (
        P("ctx", None),
        P(),
        P(None, None, "head"),
        P(),
        P(None, "head"),
        P("head"),
        P("head"),
        P("head"),
        P(None, "head"),
        P(),
        P("head", None),
    )
    return jax.shard_map(
        on_device, mesh=mesh, in_specs=placed, out_specs=P(("ctx", "head"), None), check_vma=False
    )
```

```python
import jax
import jax.numpy as jnp
from jax import lax
from jax.experimental import pallas as pl
from jax.experimental.pallas import tpu as pltpu
from jax.sharding import PartitionSpec as P

MESH = pl.DeviceIdType.MESH
F32 = jnp.float32
BF16 = jnp.bfloat16
BLOCK = 256
STATE = 128
HEAD = 64
CTX = 16
GROUP = 8
MESSAGE = STATE + 16
LOG2E = 1.4426950408889634
epsilon = 1e-05


def dot(a, b):
    return jnp.dot(a, b, preferred_element_type=F32)


def dot_rows(a, b):
    return lax.dot_general(a, b, (((1,), (1,)), ((), ())), preferred_element_type=F32)


def halves(v):
    high = v.astype(BF16)
    return high, (v - high.astype(F32)).astype(BF16)


def silu(v):
    half = 0.5 * v
    return half + half * jnp.tanh(half)


def softplus(v):
    return jnp.maximum(v, 0.0) + jnp.log1p(jnp.exp(-jnp.abs(v)))


def iotas(shape):
    return lax.broadcasted_iota(jnp.int32, shape, 0), lax.broadcasted_iota(jnp.int32, shape, 1)


def remote(src, dst, send, recv, ctx, head):
    return pltpu.make_async_remote_copy(
        src_ref=src, dst_ref=dst, send_sem=send, recv_sem=recv,
        device_id=(ctx, head), device_id_type=MESH,
    )


def kernel(
    hid, gain, wzx, wbc_hbm, wdt, bias_in, rate_in, skip_in, conv_x, conv_bc, wout, out,
    hbuf, wX, wZ, wo, st, scl, dtb, vb, btb, cb, cum, raw, lateb, endb, ec, ent, prow, ins,
    state, arow, xs, xa, msg, rmsg, cbuf, rbuf, acc, low, upp, spread, mean, flip, gates, wbc, skips, wC, sc,
    hs, ha, ys, ya, hmsg, hrmsg, xmsg, fmsg, frmsg, wsem, hsem, osem, wsend, wrecv, halo_send, halo_recv, ssend, srecv, csend, crecv,
):
    blocks = hbuf.shape[0]
    inner = vb.shape[3]
    heads = inner // HEAD
    width = inner + STATE
    ctx = lax.axis_index("ctx")
    me = lax.axis_index("head")
    core = lax.rem(ctx, 2)

    barrier = pltpu.get_barrier_semaphore()
    ctx_peers = [lax.rem(ctx + 1, CTX), lax.rem(ctx + CTX - 1, CTX)]
    for k in range(2):
        bit = lax.rem(lax.div(ctx, 2**k), 2)
        ctx_peers.append(ctx + (1 - 2 * bit) * 2**k)
    ctx_peers.extend(lax.rem(ctx + 4 * d, CTX) for d in range(1, 4))
    head_peers = [lax.rem(me + d, GROUP) for d in range(1, GROUP)]
    for peer in ctx_peers:
        pl.semaphore_signal(barrier, inc=1, device_id=(peer, me), device_id_type=MESH)
    for peer in head_peers:
        pl.semaphore_signal(barrier, inc=1, device_id=(ctx, peer), device_id_type=MESH)

    def load(b):
        return pltpu.make_async_copy(
            hid.at[pl.ds(pl.multiple_of(b * BLOCK, BLOCK), BLOCK), :], hbuf.at[b], hsem.at[b]
        )

    weights = [
        pltpu.make_async_copy(wbc_hbm.at[span, :], wbc.at[span, :], wsem.at[j])
        for j, span in enumerate(
            pl.ds(n * BLOCK, BLOCK) for n in range(wzx.shape[0] // BLOCK)
        )
    ]
    for copy in weights:
        copy.start()
    for b in (blocks - 1, *range(blocks - 1)):
        load(b).start()
    own = pltpu.make_async_copy(wout, wo.at[me], osem.at[0])
    own.start()

    r0, c0 = iotas((BLOCK, BLOCK))
    low[...] = (r0 >= c0).astype(BF16)
    upp[...] = (r0 <= c0).astype(BF16)
    flip[...] = (r0 + c0 == BLOCK - 1).astype(BF16)
    lane_head = c0 // HEAD
    q0 = lax.rem(r0, 128)
    for s in range(2):
        spread[s] = (q0 == lane_head + s * heads).astype(BF16)
    mean[...] = jnp.where(r0 // HEAD == lane_head, 1.0 / HEAD, 0.0).astype(BF16)

    lane = lax.broadcasted_iota(jnp.int32, (1, 128), 1)
    wide_lane = lax.broadcasted_iota(jnp.int32, (1, inner), 1)
    rate = jnp.zeros((1, 128), F32)
    bias = jnp.zeros((1, 128), F32)
    skip = jnp.zeros((1, inner), F32)
    for h in range(heads):
        taken = (lane == h) | (lane == heads + h)
        rate = jnp.where(taken, rate_in[h] * (-LOG2E), rate)
        bias = jnp.where(taken, bias_in[h], bias)
        skip = jnp.where(wide_lane // HEAD == h, skip_in[h], skip)
    skips[...] = jnp.broadcast_to(skip, skips.shape)

    acc[0:128, :] = jnp.zeros((128, acc.shape[1]), F32)
    pieces = wX.shape[0] // BLOCK
    def prepare(j, carry):
        span = pl.ds(pl.multiple_of(j * BLOCK, BLOCK), BLOCK)
        back = pl.ds(pl.multiple_of((pieces - 1 - j) * BLOCK, BLOCK), BLOCK)
        pltpu.make_async_copy(wbc_hbm.at[span, :], wbc.at[span, :], wsem.at[j]).wait()
        lines = [gain[pl.ds(2 * j + t, 1), :] for t in range(2)]
        column = jnp.concatenate(
            [jnp.broadcast_to(line, (128, 128)).T for line in lines], axis=0
        )
        gz = (wzx[span, :].astype(F32) * jnp.concatenate([column] * 4, axis=1)).astype(BF16)
        gbc = (wbc[span, :].astype(F32) * jnp.concatenate([column] * 2, axis=1)).astype(BF16)
        gx = jnp.concatenate([gz[:, inner:], gbc], axis=1)
        turned = dot(flip[...], jnp.concatenate([gx, gz[:, :inner]], axis=1)).astype(BF16)
        wX[span, :width] = gx[:, :width]
        wX[back, width : 2 * width] = turned[:, :width]
        wC[span, :STATE] = gx[:, width:]
        wC[back, STATE:] = turned[:, width : width + STATE]
        wZ[span, :inner] = gz[:, :inner]
        wZ[back, inner:] = turned[:, width + STATE :]
        gdt = (wdt[:, span].astype(F32) * jnp.concatenate(lines, axis=1)).astype(BF16)
        acc[0:heads, span] = gdt.astype(F32)
        acc[heads : 2 * heads, back] = dot(gdt, flip[...])
        return carry

    lax.fori_loop(0, pieces, prepare, 0)
    for j in range(wX.shape[0] // 128):
        span = slice(j * 128, (j + 1) * 128)
        wX[span, 2 * width :] = acc[0:128, span].T.astype(BF16)

    partner = ctx_peers[2]
    across = me + 1 - 2 * lax.rem(me, 2)
    up = lax.rem(me + 2, GROUP)
    down = lax.rem(me + GROUP - 2, GROUP)
    onward = lax.rem(me + 2 + core * 4, GROUP)
    origin = lax.rem(me + 6 - core * 4, GROUP)

    def other(h):
        return h + 1 - 2 * lax.rem(h, 2)

    far = lax.rem(me + 4, GROUP)
    part = pl.ds(pl.multiple_of(core * (inner // 2), 128), inner // 2)
    rest_part = pl.ds(pl.multiple_of((1 - core) * (inner // 2), 128), inner // 2)
    mine_half = wout.at[part, :]
    sources = [across, down, up, other(down), other(up), far, other(far)]

    def slot_copy(src, k, source_here, ctx_to, head_to, send_index):
        return remote(src, wo.at[source_here, part], wsend.at[send_index], wrecv.at[k], ctx_to, head_to)

    w1 = [
        slot_copy(mine_half, 0, me, ctx, across, 0),
        slot_copy(mine_half, 1, me, ctx, up, 1),
        slot_copy(mine_half, 2, me, ctx, down, 2),
    ]
    w2 = [
        slot_copy(wo.at[across, part], 3, across, ctx, up, 3),
        slot_copy(wo.at[across, part], 4, across, ctx, down, 4),
    ]
    w3 = [
        slot_copy(wo.at[origin, part], 5, origin, ctx, onward, 5),
        slot_copy(wo.at[other(origin), part], 6, other(origin), ctx, onward, 6),
    ]
    w4 = [
        remote(wo.at[h, part], wo.at[h, part], wsend.at[7 + k], wrecv.at[7 + k], partner, me)
        for k, h in enumerate(sources)
    ]

    def arrived(k):
        remote(mine_half, wo.at[sources[k], part], wsend.at[0], wrecv.at[k], ctx, me).wait_recv()

    def partner_arrived(k):
        h = sources[k]
        remote(wo.at[h, part], wo.at[h, rest_part], wsend.at[0], wrecv.at[7 + k], partner, me).wait_recv()

    def first_rows():
        return [
            remote(
                st.at[0, blocks, :, pl.ds(0, 8), :], st.at[0, 0, :, pl.ds(0, 8), :],
                halo_send.at[0], halo_recv.at[0], ctx_peers[0], me,
            ),
            remote(
                st.at[1, 0, :, pl.ds(BLOCK, 8), :], st.at[1, blocks, :, pl.ds(BLOCK, 8), :],
                halo_send.at[1], halo_recv.at[1], ctx_peers[1], me,
            ),
        ]

    def map_rows():
        return [
            remote(
                sc.at[0, blocks, pl.ds(0, 8), :], sc.at[0, 0, pl.ds(0, 8), :],
                halo_send.at[2], halo_recv.at[2], ctx_peers[0], me,
            ),
            remote(
                sc.at[1, 0, pl.ds(BLOCK, 8), :], sc.at[1, blocks, pl.ds(BLOCK, 8), :],
                halo_send.at[3], halo_recv.at[3], ctx_peers[1], me,
            ),
        ]

    def convolve(source, shape_taps, s):
        total = None
        for k in range(4):
            shift = 5 + k if s == 0 else 3 - k
            term = (0.5 * shape_taps[k : k + 1, :]) * source[shift : shift + BLOCK, :]
            total = term if total is None else total + term
        return total + total * jnp.tanh(total)

    def settle(b):
        dt = softplus(raw[b])
        dtb[b] = dt
        parts = jnp.concatenate(halves(dt * rate), axis=1)
        ahead = dot(low[...], parts)
        behind = dot(upp[...], parts)
        forward = lax.broadcasted_iota(jnp.int32, (BLOCK, 128), 1) < heads
        c = jnp.where(
            forward, ahead[:, :128] + ahead[:, 128:], behind[:, :128] + behind[:, 128:]
        )
        cum[b] = c
        end = jnp.where(forward[0:1, :], c[BLOCK - 1 : BLOCK, :], c[0:1, :])
        lateb[b] = jnp.concatenate(halves(dt * jnp.exp2(end - c)), axis=1)
        endb[b] = jnp.concatenate(halves(jnp.broadcast_to(jnp.exp2(end), (16, 128))), axis=1)

    def project(i, carry):
        b = lax.rem(i + blocks - 1, blocks)
        load(b).wait()
        h = hbuf[b]
        hf = h.astype(F32)
        scale = lax.rsqrt(jnp.sum(hf * hf, axis=1, keepdims=True) / h.shape[1] + epsilon)
        ahead = dot(h, wX[:, :width]) * scale
        p = dot(h, wX[:, width:])
        behind = p[:, :width] * scale
        for t in range(width // 128):
            at = slice(t * 128, (t + 1) * 128)
            st[0, b, t, 8:, :] = ahead[:, at]
            st[0, b + 1, t, 0:8, :] = ahead[BLOCK - 8 :, at]
            st[1, b + 1, t, :BLOCK, :] = behind[:, at]
            st[1, b, t, BLOCK:, :] = behind[0:8, at]
        raw[b] = p[:, width:] * scale + bias
        scl[b] = jnp.broadcast_to(scale, (BLOCK, 128))

        @pl.when(i == 1)
        def _():
            pl.semaphore_wait(barrier, len(ctx_peers) + len(head_peers))
            for copy in first_rows() + w1:
                copy.start()

        return carry

    lax.fori_loop(0, blocks, project, 0)

    def settle_two(i, carry):
        for u in range(4):
            settle(4 * i + u)
        return carry

    lax.fori_loop(0, blocks // 4, settle_two, 0)

    for copy in first_rows():
        copy.wait_recv()
    st[0, 0, :, 0:8, :] = jnp.where(ctx == 0, 0.0, st[0, 0, :, 0:8, :])
    st[1, blocks, :, BLOCK:, :] = jnp.where(ctx == CTX - 1, 0.0, st[1, blocks, :, BLOCK:, :])

    state[...] = jnp.zeros_like(state)
    arow[...] = jnp.ones_like(arow)

    def local(i, carry):
        @pl.when(i == 6)
        def _():
            arrived(0)
            for copy in w2 + w4[:1]:
                copy.start()

        for s in range(2):
            b = i if s == 0 else blocks - 1 - i
            x = jnp.concatenate(
                [
                    convolve(st.at[s, b + s, t], conv_x[:, t * 128 : (t + 1) * 128], s)
                    for t in range(inner // 128)
                ],
                axis=1,
            )
            bt = convolve(st.at[s, b + s, inner // 128], conv_bc[:, :STATE], s).T.astype(BF16)
            btb[s, b] = bt
            vb[s, b] = x.astype(BF16)
            late = dot(lateb[b], spread[s])
            decay = dot(endb[b], spread[s])[0:1, :]
            ends = dot(bt, (x * late).astype(BF16))
            held = state[s]
            ent[s, b] = held
            state[s] = decay * held + ends
            before = arow[s, 0:1, :]
            prow[s, b] = jnp.broadcast_to(before, (8, inner))
            arow[s] = jnp.broadcast_to(before * decay, (8, inner))
        return carry

    lax.fori_loop(0, blocks, local, 0)

    xs[...] = jnp.zeros_like(xs)
    xa[...] = jnp.ones_like(xa)

    half = pl.ds(pl.multiple_of(core * 128, 128), 128)
    other_half = pl.ds(pl.multiple_of((1 - core) * 128, 128), 128)

    def packed(row):
        line = lax.broadcasted_iota(jnp.int32, (16, row.shape[1]), 0)
        high, rest = halves(row)
        return jnp.where(
            line == 0, high.astype(F32), jnp.where(line == 1, rest.astype(F32), 0.0)
        ).astype(BF16)

    def unpacked(tail):
        tail = tail.astype(F32)
        return tail[0:1, :] + tail[1:2, :]

    def joined(k, s, theirs, factor, now, now_a, before, before_a):
        earlier = lax.rem(lax.div(ctx, 2**k), 2) == 1 - s
        mine, reach = now_a[s, 0:1, :], before_a[s, 0:1, :]
        state_now = now[s]
        before[s] = jnp.where(earlier, reach * theirs + before[s], before[s])
        before_a[s] = jnp.broadcast_to(
            jnp.where(earlier, reach * factor, reach), before_a.shape[1:]
        )
        now[s] = jnp.where(earlier, mine * theirs + state_now, factor * state_now + theirs)
        now_a[s] = jnp.broadcast_to(mine * factor, now_a.shape[1:])

    place = lax.div(ctx, 4)
    swap = remote(msg, rmsg, ssend.at[0], srecv.at[0], ctx_peers[2], me)
    pairs = remote(hmsg.at[0], hrmsg.at[0], ssend.at[1], srecv.at[1], ctx_peers[3], me)
    along = [
        remote(
            hmsg.at[1, lax.div(place + d, 4)], xmsg.at[d - 1],
            ssend.at[1 + d], srecv.at[1 + d], ctx_peers[3 + d], me,
        )
        for d in range(1, 4)
    ]
    give = remote(fmsg, frmsg, ssend.at[5], srecv.at[5], ctx_peers[2], me)

    for s in range(2):
        msg[s, :STATE, :] = state[s].astype(BF16)
        msg[s, STATE:, :] = packed(arow[s, 0:1, :])
    swap.start()

    def fill_half(k):
        for s in range(2):
            hmsg[k, s, :STATE, :] = hs[s].astype(BF16)
            hmsg[k, s, STATE:, :] = packed(ha[s, 0:1, :])

    def merge_swap():
        swap.wait_recv()
        for s in range(2):
            theirs = rmsg[s, :STATE, :].astype(F32)
            joined(0, s, theirs, unpacked(rmsg[s, STATE:, :]), state, arow, xs, xa)
            hs[s] = state[s, :, half]
            ha[s] = arow[s, :, half]
        ys[...] = jnp.zeros_like(ys)
        ya[...] = jnp.ones_like(ya)
        fill_half(0)
        pairs.start()

    def merge_pairs():
        pairs.wait_recv()
        for s in range(2):
            theirs = hrmsg[0, s, :STATE, :].astype(F32)
            joined(1, s, theirs, unpacked(hrmsg[0, s, STATE:, :]), hs, ha, ys, ya)
        fill_half(1)
        for copy in along:
            copy.start()

    def merge_along():
        for copy in along:
            copy.wait_recv()
        for s in range(2):
            far_state = jnp.zeros((STATE, 128), F32)
            for d in (3, 2, 1) if s == 0 else (1, 2, 3):
                used = place >= d if s == 0 else place < d
                factor = unpacked(xmsg[d - 1, STATE:, :])
                theirs = xmsg[d - 1, :STATE, :].astype(F32)
                far_state = jnp.where(used, factor * far_state + theirs, far_state)
            ys[s] = ya[s, 0:1, :] * far_state + ys[s]
        fmsg[...] = ys[...].astype(BF16)
        give.start()

    def merge_give():
        give.wait_recv()
        for s in range(2):
            xs[s, :, half] = xa[s, 0:1, half] * ys[s] + xs[s, :, half]
            xs[s, :, other_half] = (
                xa[s, 0:1, other_half] * frmsg[s].astype(F32) + xs[s, :, other_half]
            )

    def project_maps(i, carry):
        b = lax.rem(i + blocks - 1, blocks)
        p = dot(hbuf[b], wC[...])
        scale = scl[b]
        ahead = p[:, :STATE] * scale
        sc[0, b, 8:, :] = ahead
        sc[0, b + 1, 0:8, :] = ahead[BLOCK - 8 :, :]
        behind = p[:, STATE:] * scale
        sc[1, b + 1, :BLOCK, :] = behind
        sc[1, b, BLOCK:, :] = behind[0:8, :]

        @pl.when(i == 2)
        def _():
            for copy in map_rows():
                copy.start()

        @pl.when(i == 6)
        def _():
            merge_swap()

        return carry

    lax.fori_loop(0, blocks, project_maps, 0)

    def within(step, carry):
        i = lax.rem(step + 1, blocks)

        @pl.when(step == 4)
        def _():
            for k in range(1, 5):
                arrived(k)
            for copy in w3 + w4[1:5]:
                copy.start()

        @pl.when(step == 3)
        def _():
            merge_pairs()

        @pl.when(step == blocks - 2)
        def _():
            for copy in map_rows():
                copy.wait_recv()
            sc[0, 0, 0:8, :] = jnp.where(ctx == 0, 0.0, sc[0, 0, 0:8, :])
            sc[1, blocks, BLOCK:, :] = jnp.where(ctx == CTX - 1, 0.0, sc[1, blocks, BLOCK:, :])

        dt_pair = jnp.concatenate(halves(dtb[i]), axis=1)
        first, second = iotas((128, 128))
        side = second < HEAD
        for s in range(2):
            c = cum[i]
            maps = convolve(sc.at[s, i + s], conv_bc[:, STATE:], s).astype(BF16)
            cb[s, i] = maps
            ec[s, i] = dot(jnp.concatenate(halves(jnp.exp2(c)), axis=1), spread[s])
            weighted = (vb[s, i].astype(F32) * dot(dt_pair, spread[s])).astype(BF16)
            keep = first >= second if s == 0 else first <= second
            scores = dot(maps, btb[s, i])
            corner = [
                jnp.where(keep, scores[:128, :128], 0.0),
                jnp.where(keep, scores[128:, 128:], 0.0),
            ]
            cross = scores[128:, :128] if s == 0 else scores[:128, 128:]
            turned = c.T
            for pair in range(heads // 2):
                at = slice(pair * 128, (pair + 1) * 128)
                short, long = [], []
                for t in range(2):
                    lane = s * heads + pair * 2 + t
                    down_col = [c[:128, lane : lane + 1], c[128:, lane : lane + 1]]
                    row = turned[lane : lane + 1, :]
                    over = [row[:, :128], row[:, 128:]]
                    square = [
                        (corner[q] * jnp.exp2(jnp.minimum(down_col[q] - over[q], 0.0))).astype(BF16)
                        for q in range(2)
                    ]
                    far_off = (cross * jnp.exp2(down_col[1 - s] - over[s])).astype(BF16)
                    short.append(square[s])
                    long.extend([far_off, square[1]] if s == 0 else [square[0], far_off])
                w = weighted[:, at]
                w_rows = [w[:128, :], w[128:, :]]
                zero = jnp.zeros_like(w_rows[0])
                first_head = [jnp.where(side, v, zero) for v in w_rows]
                second_head = [jnp.where(side, zero, v) for v in w_rows]
                brief = dot(
                    jnp.concatenate(short, axis=1),
                    jnp.concatenate([first_head[s], second_head[s]], axis=0),
                )
                full = dot(
                    jnp.concatenate(long, axis=1), jnp.concatenate(first_head + second_head, axis=0)
                )
                result = [brief, full] if s == 0 else [full, brief]
                for q in range(2):
                    down_rows = slice(q * 128, (q + 1) * 128)
                    ins[s, i, down_rows, at] = result[q] + skips[0:1, at] * vb[
                        s, i, down_rows, at
                    ].astype(F32)
        return carry

    lax.fori_loop(0, blocks, within, 0)
    def make_gate(b, slot):
        scale = jnp.concatenate([scl[b]] * (inner // 128), axis=1)
        h = hbuf[b]
        for s in range(2):
            gates[slot, s] = silu(dot(h, wZ[:, s * inner : (s + 1) * inner]) * scale)

    merge_along()
    make_gate(lax.rem(me + 1, blocks), 0)
    merge_give()

    def finish(i, carry):
        b = lax.rem(me + 1 + i, blocks)
        both = jnp.zeros((BLOCK, inner), F32)
        for s in range(2):
            whole = (ent[s, b] + prow[s, b][0:1, :] * xs[s]).astype(BF16)
            result = ins[s, b] + ec[s, b] * dot(cb[s, b], whole)
            gated = result * gates[lax.rem(i, 2), s]
            power = dot((gated * gated).astype(BF16), mean[...])
            both = both + gated * lax.rsqrt(power + epsilon)
        cbuf[b] = both.astype(BF16)

        @pl.when(i == 4)
        def _():
            for k in (5, 6):
                arrived(k)
            for copy in w4[5:]:
                copy.start()

        @pl.when(i < blocks - 1)
        def _():
            remote(cbuf.at[b], rbuf.at[me], csend.at[b], crecv.at[me], ctx, b).start()

        make_gate(lax.rem(me + 2 + i, blocks), lax.rem(i + 1, 2))
        return carry

    lax.fori_loop(0, blocks, finish, 0)

    own.wait()
    for k in range(7):
        partner_arrived(k)

    acc[...] = hbuf[me].astype(F32)

    def multiply(block, j):
        acc[...] += dot(block, wo[j])

    multiply(cbuf[me], me)

    def gathered(i, carry):
        j = lax.rem(me + blocks - 1 - i, blocks)
        remote(cbuf.at[j], rbuf.at[j], csend.at[j], crecv.at[j], ctx, j).wait_recv()
        multiply(rbuf[j], j)
        return carry

    lax.fori_loop(0, blocks - 1, gathered, 0)
    out[...] = acc[...].astype(BF16)

    for copy in w1 + w2 + w3 + w4 + first_rows() + map_rows() + [swap, pairs, give] + along:
        copy.wait_send()

    def drained(i, carry):
        j = lax.rem(me + 1 + i, blocks)
        remote(cbuf.at[j], rbuf.at[me], csend.at[j], crecv.at[me], ctx, j).wait_send()
        return carry

    lax.fori_loop(0, blocks - 1, drained, 0)


def on_device(
    hidden, norm_gain, w_zx, w_bc, w_dt, dt_bias, decay_rate, skip_gain, conv_x, conv_bc, w_out
):
    amount, wide = hidden.shape
    inner = conv_x.shape[1]
    heads = w_dt.shape[1]
    width = inner + STATE
    blocks = amount // BLOCK
    vmem = pl.BlockSpec(memory_space=pltpu.VMEM)
    hbm = pl.BlockSpec(memory_space=pl.ANY)
    smem = pl.BlockSpec(memory_space=pltpu.SMEM)
    dma = pltpu.SemaphoreType.DMA
    return pl.pallas_call(
        kernel,
        out_shape=pltpu.VMEM((BLOCK, wide), BF16),
        in_specs=[hbm, vmem, vmem, hbm, vmem, smem, smem, smem, vmem, vmem, hbm],
        out_specs=vmem,
        scratch_shapes=[
            pltpu.VMEM((blocks, BLOCK, wide), BF16),
            pltpu.VMEM((wide, 2 * width + 128), BF16),
            pltpu.VMEM((wide, 2 * inner), BF16),
            pltpu.VMEM((GROUP, inner, wide), BF16),
            pltpu.VMEM((2, blocks + 1, width // 128, BLOCK + 8, 128), F32),
            pltpu.VMEM((blocks, BLOCK, 128), F32),
            pltpu.VMEM((blocks, BLOCK, 128), F32),
            pltpu.VMEM((2, blocks, BLOCK, inner), BF16),
            pltpu.VMEM((2, blocks, STATE, BLOCK), BF16),
            pltpu.VMEM((2, blocks, BLOCK, STATE), BF16),
            pltpu.VMEM((blocks, BLOCK, 128), F32),
            pltpu.VMEM((blocks, BLOCK, 128), F32),
            pltpu.VMEM((blocks, BLOCK, 256), BF16),
            pltpu.VMEM((blocks, 16, 256), BF16),
            pltpu.VMEM((2, blocks, BLOCK, inner), F32),
            pltpu.VMEM((2, blocks, STATE, inner), F32),
            pltpu.VMEM((2, blocks, 8, inner), F32),
            pltpu.VMEM((2, blocks, BLOCK, inner), F32),
            pltpu.VMEM((2, STATE, inner), F32),
            pltpu.VMEM((2, 8, inner), F32),
            pltpu.VMEM((2, STATE, inner), F32),
            pltpu.VMEM((2, 8, inner), F32),
            pltpu.VMEM((2, MESSAGE, inner), BF16),
            pltpu.VMEM((2, MESSAGE, inner), BF16),
            pltpu.VMEM((GROUP, BLOCK, inner), BF16),
            pltpu.VMEM((GROUP, BLOCK, inner), BF16),
            pltpu.VMEM((BLOCK, wide), F32),
            pltpu.VMEM((BLOCK, BLOCK), BF16),
            pltpu.VMEM((BLOCK, BLOCK), BF16),
            pltpu.VMEM((2, BLOCK, BLOCK), BF16),
            pltpu.VMEM((BLOCK, BLOCK), BF16),
            pltpu.VMEM((BLOCK, BLOCK), BF16),
            pltpu.VMEM((2, 2, BLOCK, inner), F32),
            pltpu.VMEM((wide, 2 * STATE), BF16),
            pltpu.VMEM((8, inner), F32),
            pltpu.VMEM((wide, 2 * STATE), BF16),
            pltpu.VMEM((2, blocks + 1, BLOCK + 8, STATE), F32),
            pltpu.VMEM((2, STATE, 128), F32),
            pltpu.VMEM((2, 8, 128), F32),
            pltpu.VMEM((2, STATE, 128), F32),
            pltpu.VMEM((2, 8, 128), F32),
            pltpu.VMEM((2, 2, MESSAGE, 128), BF16),
            pltpu.VMEM((1, 2, MESSAGE, 128), BF16),
            pltpu.VMEM((3, MESSAGE, 128), BF16),
            pltpu.VMEM((2, STATE, 128), BF16),
            pltpu.VMEM((2, STATE, 128), BF16),
            dma((wide // BLOCK,)),
            dma((blocks,)),
            dma((1,)),
            dma((14,)),
            dma((14,)),
            dma((4,)),
            dma((4,)),
            dma((6,)),
            dma((6,)),
            dma((GROUP,)),
            dma((GROUP,)),
        ],
        compiler_params=pltpu.CompilerParams(
            collective_id=0, has_side_effects=True, vmem_limit_bytes=56 * 1024 * 1024
        ),
    )(
        hidden,
        norm_gain.reshape(8, wide // 8),
        pltpu.with_memory_space_constraint(w_zx.reshape(wide, 2 * inner), pltpu.VMEM),
        w_bc,
        w_dt.T,
        dt_bias,
        decay_rate,
        skip_gain,
        conv_x,
        conv_bc,
        w_out,
    )


def solution(mesh):
    placed = (
        P("ctx", None),
        P(),
        P(None, None, "head"),
        P(),
        P(None, "head"),
        P("head"),
        P("head"),
        P("head"),
        P(None, "head"),
        P(),
        P("head", None),
    )
    return jax.shard_map(
        on_device, mesh=mesh, in_specs=placed, out_specs=P(("ctx", "head"), None), check_vma=False
    )
```
